256 devices in a mesh: bins: 16 (over y, z_hi, core), batch: 16 (over x, z_lo).
Axes of the slice: x: 4, y: 4, z: 8 (z_hi: 2, z_lo: 4; z = z_hi * 4 + z_lo), core: 2. Of those that a mesh axis runs over, the one named last changes fastest.
Arguments:
- features: bfloat16 [16, 4096, 1536], P('batch', 'bins'), may hold values from -6 to 6
- norm_gain: float32 [1536], replicated, may hold values from 0.25 to 1.75
- convolution_taps_weight: bfloat16 [3, 1536, 768], replicated, may hold values from -0.09375 to 0.09375
- out_weight: bfloat16 [768, 1536], replicated, may hold values from -0.21875 to 0.21875
- head_weight: bfloat16 [1536, 4096], P(None, 'batch'), may hold values from -0.15625 to 0.15625
- rc_perm: int32 [1536], replicated, may hold values from 0 to 1535, each once
- exon_bins: int32 [16, 64, 8], P('batch'), may hold values from 0 to 4095, as said below
- exon_count: int32 [16, 64], P('batch'), may hold values from 1 to 8
- gene_strand: int32 [16, 64], P('batch'), may hold values 0 or 1
- gene_target: float32 [16, 64, 4096], P('batch', 'bins'), may hold values from 0.5 to 8
Outputs:
- input_grad: bfloat16 [16, 4096, 1536], P('batch', 'bins')
- out_weight_grad: float32 [768, 1536], P('batch')
The draws below stay inside these ranges and needn't reach their ends.
Inputs may be any that keep to these rules, and one draw needn't show every extreme that they name: `rc_perm`: a permutation of the channels. `exon_bins`: bins of the gene's own sequence; a bin may be listed more than once; each gene's listed bins lie within 256 consecutive bins. All genes of a sequence may lie within the same 256 bins j * 256 to (j + 1) * 256 - 1 of one j, and then every one of those bins may be listed and counted.
All inputs are finite; a program needn't handle non-finite values. No bound on the sum of `gene_strand` on one device may be relied on, other than what follows from the above.
Results may differ from the reference program's by a relative error of at most 0.014.
Values may be sent and summed in bfloat16 or wider, within the bound.
No kernel may reach another device: no remote copies, remote signals or barrier semaphores. Data moves between devices by JAX's collectives and lax.ppermute only.
A program may use at most 128 MiB of HBM per device.

```python
import math
import jax
import jax.numpy as jnp
from jax import lax

C = 1536
H = 768
TR = 4096
DILATION_STEP = 16
EX = 8
LB = 256
L = 4096
G = 64
SEQS = 16


def exon_layout(key):
    folded = jax.random.fold_in(key, 911)
    key_list = jax.random.split(folded, 6)
    starts = jax.random.randint(key_list[0], (SEQS, G, 1), 0, L - LB + 1)
    offsets = jax.random.randint(key_list[1], (SEQS, G, EX), 0, LB)
    spread = starts + offsets
    chosen_sequence = jax.random.randint(key_list[2], (), 0, SEQS)
    chosen_block = jax.random.randint(key_list[3], (), 0, L // LB)
    rotation = jax.random.randint(key_list[4], (), 0, LB)
    listed = jnp.arange(G * EX, dtype=jnp.int32).reshape(G, EX)
    packed = (listed + rotation) % LB + chosen_block * LB
    clustered = jnp.arange(SEQS, dtype=jnp.int32) == chosen_sequence
    exon_list = jnp.where(clustered[:, None, None], packed[None, :, :], spread).astype(jnp.int32)
    counted = jax.random.randint(key_list[5], (SEQS, G), 1, EX + 1)
    counted = jnp.where(clustered[:, None], EX, counted).astype(jnp.int32)
    return (exon_list, counted)


def draw_exon_bins(key, part):
    return exon_layout(key)[0]


def draw_exon_count(key, part):
    return exon_layout(key)[1]


def with_ends(drawn, stream_key, low, top_value):
    longest = drawn.shape.index(max(drawn.shape))
    spots = []
    for shift in (0, 1):
        where = [jax.random.randint(jax.random.fold_in(stream_key, axis), (), 0, length) for axis, length in enumerate(drawn.shape)]
        where[longest] = (where[longest] + shift) % drawn.shape[longest]
        spots.append(tuple(where))
    return drawn.at[spots[0]].set(low).at[spots[1]].set(top_value)


def level_of(rng, shape, cuts, least, high):
    def one(position, blocks):
        heights = jax.random.uniform(jax.random.fold_in(jax.random.fold_in(rng, 6), position), (blocks,), jnp.float32, least / len(cuts), high / len(cuts))
        return jnp.repeat(jnp.exp(heights), shape[position] // blocks).reshape((-1,) + (1,) * (len(shape) - position - 1))

    level = one(*cuts[0])
    for cut in cuts[1:]:
        level = level * one(*cut)
    return level


def scatter_about(key, dims, scale, limit, cuts=(), kind=jnp.bfloat16):
    factor_of = level_of(key, dims, cuts, -0.22, 0.18) if cuts else 1.0
    drawn = jax.random.normal(key, dims, jnp.float32) * scale * factor_of
    return jnp.minimum(jnp.maximum(drawn, -limit), limit).astype(kind)


def setup_inputs(seed: int = 0) -> dict:
    streams_of = jax.random.split(jax.random.key(seed), 11)
    features = scatter_about(streams_of[0], (SEQS, L, C), 1.0, 6.0, ((0, 16), (1, 16)))
    norm_gain = jnp.clip(1.0 + 0.15 * jax.random.normal(streams_of[1], (C,), jnp.float32), 0.25, 1.75)
    convolution_taps_weight = scatter_about(streams_of[2], (3, C, H), (3 * C) ** -0.5, 0.09375)
    out_weight = scatter_about(streams_of[3], (H, C), H ** -0.5, 0.21875)
    head_weight = scatter_about(streams_of[4], (C, TR), C ** -0.5, 0.15625, ((1, 16),))
    rc_perm = jax.random.permutation(streams_of[5], C).astype(jnp.int32)
    exon_bins = draw_exon_bins(jax.random.fold_in(streams_of[10], 71), 0)
    exon_count = draw_exon_count(jax.random.fold_in(streams_of[10], 71), 0)
    gene_strand = with_ends((jax.random.randint(streams_of[8], (SEQS, G), 0, 2) < 1).astype(jnp.int32), jax.random.fold_in(streams_of[8], 1), 0, 1)
    gene_target = jnp.clip(jnp.exp(math.log(8.0) - 2.7725887 * jax.random.uniform(streams_of[9], (SEQS, G, TR), jnp.float32) ** level_of(streams_of[9], (SEQS, G, TR), ((0, 16), (1, 16)), -0.2, 0.2)), 0.5, 8.0)
    return dict(features=features, norm_gain=norm_gain, convolution_taps_weight=convolution_taps_weight, out_weight=out_weight, head_weight=head_weight, rc_perm=rc_perm, exon_bins=exon_bins, exon_count=exon_count, gene_strand=gene_strand, gene_target=gene_target)


def gelu_slope(argument):
    return 0.5 * (1.0 + jax.scipy.special.erf(argument * 0.7071067811865476)) + argument * jnp.exp(-0.5 * argument * argument) * 0.3989422804014327

def pair_flip(matrix, strand):
    swapped = matrix.reshape(matrix.shape[0], -1, 2)[:, :, ::-1].reshape(matrix.shape)
    return jnp.where(strand[:, None] == 1, swapped, matrix)

def exon_hits(bin_lists, counts, positions):
    listed = jnp.arange(bin_lists.shape[1], dtype=jnp.int32)[None, :] < counts[:, None]
    matched = (bin_lists[:, :, None] == positions[None, None, :]) & listed[:, :, None]
    return lax.optimization_barrier(jnp.sum(matched.astype(jnp.float32), axis=1)).astype(jnp.bfloat16)

def one_sequence(inputs, norm_gain, convolution_taps_weight, out_weight, head_weight, rc_perm, inverse_perm):
    features, bin_lists, counts, strand, target = inputs
    widened = features.astype(jnp.float32)
    count_of_rows = widened.shape[0]
    inverse = lax.rsqrt(lax.optimization_barrier(jnp.mean(widened * widened, axis=-1, keepdims=True)) + 1e-06)
    normed = widened * inverse * norm_gain
    hidden_state = jax.nn.gelu(normed, approximate=False).astype(jnp.bfloat16)
    padded_input = jnp.pad(hidden_state, ((DILATION_STEP, DILATION_STEP), (0, 0)))
    convolved_sum = jnp.zeros((count_of_rows, convolution_taps_weight.shape[2]), jnp.float32)
    for kernel_tap_index in range(3):
        convolved_sum = convolved_sum + jnp.dot(padded_input[kernel_tap_index * DILATION_STEP:kernel_tap_index * DILATION_STEP + count_of_rows], convolution_taps_weight[kernel_tap_index], preferred_element_type=jnp.float32)
    active = jax.nn.gelu(convolved_sum, approximate=False).astype(jnp.bfloat16)
    block_out = (widened + jnp.dot(active, out_weight, preferred_element_type=jnp.float32)).astype(jnp.bfloat16)
    logits = jnp.dot(block_out, head_weight, preferred_element_type=jnp.float32)
    predicted = jax.nn.softplus(logits).astype(jnp.bfloat16)
    positions = jnp.arange(count_of_rows, dtype=jnp.int32)
    hit_counts = exon_hits(bin_lists, counts, positions)
    partial_value = jnp.dot(hit_counts, predicted, preferred_element_type=jnp.float32)
    coverage = pair_flip(partial_value, strand)
    adjoint = (1.0 - target / (1.0 + coverage)).astype(jnp.bfloat16)
    spread_back = pair_flip(adjoint, strand)
    pred_grad = lax.dot_general(hit_counts, spread_back, (((0,), (0,)), ((), ())), preferred_element_type=jnp.float32)
    logit_grad = (pred_grad * jax.nn.sigmoid(logits)).astype(jnp.bfloat16)
    head_back = lax.dot_general(logit_grad, head_weight, (((1,), (1,)), ((), ())), preferred_element_type=jnp.float32)
    mirrored = block_out[::-1].astype(jnp.float32)
    block_wide = block_out.astype(jnp.float32)
    rc_grad = block_wide - 0.5 * (mirrored[:, rc_perm] + mirrored[:, inverse_perm])
    block_grad = (head_back + rc_grad).astype(jnp.bfloat16)
    weight_grad = lax.dot_general(active, block_grad, (((0,), (0,)), ((), ())), preferred_element_type=jnp.float32)
    activation_gradient = (lax.dot_general(block_grad, out_weight, (((1,), (1,)), ((), ())), preferred_element_type=jnp.float32) * gelu_slope(convolved_sum)).astype(jnp.bfloat16)
    padded_gradient = jnp.pad(activation_gradient, ((DILATION_STEP, DILATION_STEP), (0, 0)))
    hidden_grad = jnp.zeros((count_of_rows, convolution_taps_weight.shape[1]), jnp.float32)
    for kernel_tap_index in range(3):
        shift_amount = (2 - kernel_tap_index) * DILATION_STEP
        hidden_grad = hidden_grad + lax.dot_general(padded_gradient[shift_amount:shift_amount + count_of_rows], convolution_taps_weight[kernel_tap_index], (((1,), (1,)), ((), ())), preferred_element_type=jnp.float32)
    normed_grad = hidden_grad * gelu_slope(normed) * norm_gain
    norm_back = inverse * normed_grad - widened * inverse ** 3 * lax.optimization_barrier(jnp.mean(normed_grad * widened, axis=-1, keepdims=True))
    input_grad = (block_grad.astype(jnp.float32) + norm_back).astype(jnp.bfloat16)
    return (input_grad, weight_grad)

def reference(features, norm_gain, convolution_taps_weight, out_weight, head_weight, rc_perm, exon_bins, exon_count, gene_strand, gene_target):
    channels = rc_perm.shape[0]
    inverse_perm = jnp.zeros((channels,), jnp.int32).at[rc_perm].set(jnp.arange(channels, dtype=jnp.int32))

    def per_sequence(grad_total, inputs):
        input_grad, weight_grad = one_sequence(inputs, norm_gain, convolution_taps_weight, out_weight, head_weight, rc_perm, inverse_perm)
        return (grad_total + weight_grad, input_grad)
    start_total = jnp.zeros((out_weight.shape[0], out_weight.shape[1]), jnp.float32)
    grad_total, input_grads = lax.scan(per_sequence, start_total, (features, exon_bins, exon_count, gene_strand, gene_target))
    return (input_grads, grad_total)
```

```python
import jax
import jax.numpy as jnp
from jax import lax
from jax.sharding import Mesh
from jax.sharding import PartitionSpec as P

DILATION_STEP = 16
BINS = ("y", "zh", "core")


def shifted(block, axis, shift):
    count = lax.axis_size(axis)
    return lax.ppermute(block, axis, [(i, (i + shift) % count) for i in range(count)])


def edge_rows(block, width):
    count = lax.axis_size(BINS)
    low = lax.ppermute(block[-width:], BINS, [(i, i + 1) for i in range(count - 1)])
    high = lax.ppermute(block[:width], BINS, [(i + 1, i) for i in range(count - 1)])
    return low, high


def pick(stack, index):
    return lax.dynamic_index_in_dim(stack, index, 0, keepdims=False)


def wide(value):
    return value.astype(jnp.float32)


def narrow(value):
    return value.astype(jnp.bfloat16)


def gelu_slope(argument):
    return (
        0.5 * (1.0 + jax.scipy.special.erf(argument * 0.7071067811865476))
        + argument * jnp.exp(-0.5 * argument * argument) * 0.3989422804014327
    )


def dot(left, right, over=(1, 0)):
    return lax.dot_general(
        left, right, (((over[0],), (over[1],)), ((), ())), preferred_element_type=jnp.float32
    )


def normalize(rows, norm_gain):
    widened = wide(rows)
    inverse = lax.rsqrt(jnp.mean(widened * widened, axis=-1, keepdims=True) + 1e-06)
    normed = widened * inverse * norm_gain
    return inverse, normed, narrow(jax.nn.gelu(normed, approximate=False))


def gather_head(head_weight):
    n = lax.axis_size("zl")
    me, core = lax.axis_index("zl"), lax.axis_index("core")
    by_track = head_weight.T
    half = by_track.shape[0] // 2
    mine = pick(by_track.reshape(2, half, -1), core)
    held = jnp.zeros((n,) + mine.shape, mine.dtype)
    held = lax.dynamic_update_index_in_dim(held, mine, me, 0)
    for k in range(1, n):
        held = lax.dynamic_update_index_in_dim(held, shifted(mine, "zl", k), (me - k) % n, 0)
    both = jnp.concatenate([held, shifted(held, "core", 1)], axis=0)
    return both.reshape(2 * n * half, -1)


def deal_targets(gene_target, own_strand, own_count):
    nx, nz = lax.axis_size("x"), lax.axis_size("zl")
    x, core = lax.axis_index("x"), lax.axis_index("core")
    genes, tracks = gene_target.shape
    odd = lax.broadcasted_iota(jnp.int32, gene_target.shape, 1) % 2 == 1
    swapped = jnp.where(odd, jnp.roll(gene_target, 1, axis=1), jnp.roll(gene_target, -1, axis=1))
    flipped = jnp.where(own_strand[:, None] == 1, swapped, gene_target)
    parts = flipped.reshape(genes, nx, nz, 2, tracks // (nx * nz * 2))
    parts = jnp.transpose(parts, (1, 0, 3, 2, 4))
    parts = jnp.where(core == 0, parts, parts[:, :, ::-1])
    parts = parts.reshape(nx, genes, tracks // nx)
    counts = jnp.broadcast_to(wide(own_count)[None, :, None], (nx, genes, 128))
    parts = jnp.concatenate([parts, counts], axis=2)
    pieces = [pick(parts, x)]
    for k in range(1, nx):
        pieces.append(shifted(pick(parts, (x + k) % nx), "x", k))
    return jnp.concatenate(pieces, axis=0)


def per_device(
    features,
    norm_gain,
    convolution_taps_weight,
    out_weight,
    head_weight,
    rc_perm,
    exon_bins,
    exon_count,
    gene_strand,
    gene_target,
):
    ny, nh, nc, nx, nz = (lax.axis_size(a) for a in ("y", "zh", "core", "x", "zl"))
    y, zh, core, x, zl = (lax.axis_index(a) for a in ("y", "zh", "core", "x", "zl"))
    bin_devices = ny * nh * nc
    bin_index = (y * nh + zh) * nc + core
    rows = features[0]
    count_of_rows, channels = rows.shape
    low, high = edge_rows(rows, DILATION_STEP)
    widened = wide(rows)
    inverse, normed, hidden_own = normalize(rows, norm_gain)

    owner = lax.iota(jnp.int32, bin_devices)
    owner_core = (core + owner // (ny * nh)) % nc
    owner_y = (y + (owner // nh) % ny) % ny
    owner_zh = (zh + owner % nh) % nh
    owner = (owner_y * nh + owner_zh) * nc + owner_core
    genes, listed_most = exon_bins.shape[1:]
    own_genes = genes // bin_devices
    place = lax.broadcasted_iota(jnp.int32, (genes, listed_most), 1)
    listed = place < exon_count[0][:, None]
    entry_bins = jnp.where(listed, exon_bins[0], -1).reshape(bin_devices, -1)
    chosen = owner[:, None] == lax.iota(jnp.int32, bin_devices)[None, :]
    entry_bins = jnp.sum(jnp.where(chosen[:, :, None], entry_bins[None], 0), axis=1).reshape(-1)
    positions = bin_index * count_of_rows + lax.iota(jnp.int32, count_of_rows)
    pick_rows = narrow(entry_bins[None, :] == positions[:, None])
    entries = entry_bins.shape[0]

    own_strand = lax.dynamic_slice_in_dim(gene_strand[0], bin_index * own_genes, own_genes, 0)
    own_count = lax.dynamic_slice_in_dim(exon_count[0], bin_index * own_genes, own_genes, 0)
    targets = deal_targets(gene_target[0], own_strand, own_count)
    head = gather_head(head_weight)

    edge_hidden = normalize(jnp.concatenate([low, high], axis=0), norm_gain)[2]
    padded_input = jnp.concatenate(
        [edge_hidden[:DILATION_STEP], hidden_own, edge_hidden[DILATION_STEP:]], axis=0
    )
    convolved_sum = jnp.zeros((count_of_rows, convolution_taps_weight.shape[2]), jnp.float32)
    for tap in range(3):
        convolved_sum = convolved_sum + dot(
            padded_input[tap * DILATION_STEP : tap * DILATION_STEP + count_of_rows],
            convolution_taps_weight[tap],
        )
    active = narrow(jax.nn.gelu(convolved_sum, approximate=False))
    block_out = narrow(widened + dot(active, out_weight))

    sent = narrow(dot(pick_rows, block_out, (0, 0))).reshape(nc, ny, nh, -1, channels)
    sent = narrow(wide(sent[0]) + wide(shifted(sent[1], "core", 1)))
    sent = narrow(
        wide(sent[0]) + sum(wide(shifted(sent[k], "y", k)) for k in range(1, ny))
    )
    sent = narrow(wide(sent[0]) + wide(shifted(sent[1], "zh", 1)))
    gathered = jnp.concatenate([sent] + [shifted(sent, "x", k) for k in range(1, nx)], axis=0)

    partner = lax.ppermute(block_out, BINS, [(i, bin_devices - 1 - i) for i in range(bin_devices)])

    logits = dot(gathered, head, (1, 1))
    grouped = (nx * own_genes, listed_most, logits.shape[1])
    tracks = logits.shape[1]
    predicted = narrow(jax.nn.softplus(logits)).reshape(grouped)
    counted = lax.broadcasted_iota(jnp.int32, grouped[:2], 1) < targets[:, tracks:tracks + 1].astype(
        jnp.int32
    )
    coverage = jnp.sum(jnp.where(counted[:, :, None], wide(predicted), 0.0), axis=1)
    spread_back = narrow(1.0 - targets[:, :tracks] / (1.0 + coverage))
    logit_grad = narrow(
        wide(spread_back)[:, None, :] * jax.nn.sigmoid(logits).reshape(grouped)
    ).reshape(logits.shape)
    back = narrow(dot(logit_grad, head)).reshape(nx, -1, channels)
    back = narrow(wide(back[0]) + sum(wide(shifted(back[k], "x", -k)) for k in range(1, nx)))
    back = jnp.concatenate([back, shifted(back, "zh", 1)], axis=0)
    back = jnp.concatenate([back] + [shifted(back, "y", -k) for k in range(1, ny)], axis=0)
    back_other = shifted(back, "core", 1)
    head_back = dot(pick_rows[:, : entries // 2], back) + dot(
        pick_rows[:, entries // 2 :], back_other
    )

    count_iota = lax.broadcasted_iota(jnp.int32, (count_of_rows, count_of_rows), 0)
    reversal = narrow(count_iota + count_iota.T == count_of_rows - 1)
    channel = lax.broadcasted_iota(jnp.int32, (channels, channels), 0)
    mixing = narrow(wide(rc_perm[None, :] == channel) + wide(rc_perm[:, None] == channel.T))
    mirrored = narrow(dot(reversal, partner))
    rc_grad = wide(block_out) - 0.5 * dot(mirrored, mixing)
    block_grad = narrow(head_back + rc_grad)

    half = channels // 2
    turned = jnp.where(core == 0, block_grad, jnp.roll(block_grad, half, axis=1))
    share = dot(active, turned[:, :half], (0, 0)) + wide(
        shifted(narrow(dot(active, turned[:, half:], (0, 0))), "core", 1)
    )
    share = narrow(share).reshape(nx, -1, half)
    share = wide(pick(share, x)) + sum(
        wide(shifted(pick(share, (x + k) % nx), "x", k)) for k in range(1, nx)
    )
    share = narrow(share).reshape(nz, -1, half)
    share = wide(pick(share, zl)) + sum(
        wide(shifted(pick(share, (zl + k) % nz), "zl", k)) for k in range(1, nz)
    )
    share = narrow(share)
    share = narrow(
        (wide(share) + wide(shifted(share, "y", 2)))
        + (wide(shifted(share, "y", 1)) + wide(shifted(share, "y", 3)))
    )
    share = wide(share) + wide(shifted(share, "zh", 1))
    other = shifted(share, "core", 1)
    out_weight_grad = jnp.concatenate(
        [jnp.where(core == 0, share, other), jnp.where(core == 0, other, share)], axis=1
    )

    activation_gradient = narrow(dot(block_grad, out_weight, (1, 1)) * gelu_slope(convolved_sum))
    low, high = edge_rows(activation_gradient, DILATION_STEP)
    padded_gradient = jnp.concatenate([low, activation_gradient, high], axis=0)
    hidden_grad = jnp.zeros((count_of_rows, channels), jnp.float32)
    for tap in range(3):
        start = (2 - tap) * DILATION_STEP
        hidden_grad = hidden_grad + dot(
            padded_gradient[start : start + count_of_rows], convolution_taps_weight[tap], (1, 1)
        )
    normed_grad = hidden_grad * gelu_slope(normed) * norm_gain
    norm_back = inverse * normed_grad - widened * inverse**3 * jnp.mean(
        normed_grad * widened, axis=-1, keepdims=True
    )
    input_grad = narrow(wide(block_grad) + norm_back)
    return (input_grad[None], out_weight_grad)


def solution(mesh):
    cut = Mesh(mesh.devices.reshape(4, 2, 2, 4, 4), BINS + ("x", "zl"))
    batch = ("x", "zl")
    in_specs = (
        P(batch, BINS, None),
        P(),
        P(),
        P(),
        P(None, batch),
        P(),
        P(batch, None, None),
        P(batch, None),
        P(batch, None),
        P(batch, BINS, None),
    )
    out_specs = (P(batch, BINS, None), P(batch, None))
    return jax.shard_map(
        per_device, mesh=cut, in_specs=in_specs, out_specs=out_specs, check_vma=False
    )
```

```python
import jax
import jax.numpy as jnp
from jax import lax
from jax.experimental import pallas as pl
from jax.experimental.pallas import tpu as pltpu
from jax.sharding import Mesh
from jax.sharding import PartitionSpec as P

DILATION_STEP = 16
BINS = ("y", "zh", "core")


def shifted(block, axis, shift):
    count = lax.axis_size(axis)
    return lax.ppermute(block, axis, [(i, (i + shift) % count) for i in range(count)])


def edge_rows(block, width):
    count = lax.axis_size(BINS)
    low = lax.ppermute(block[-width:], BINS, [(i, i + 1) for i in range(count - 1)])
    high = lax.ppermute(block[:width], BINS, [(i + 1, i) for i in range(count - 1)])
    return low, high


def pick(stack, index):
    return lax.dynamic_index_in_dim(stack, index, 0, keepdims=False)


def wide(value):
    return value.astype(jnp.float32)


def narrow(value):
    return value.astype(jnp.bfloat16)


def gelu_slope(argument):
    return (
        0.5 * (1.0 + jax.scipy.special.erf(argument * 0.7071067811865476))
        + argument * jnp.exp(-0.5 * argument * argument) * 0.3989422804014327
    )


def dot(left, right, over=(1, 0)):
    return lax.dot_general(
        left, right, (((over[0],), (over[1],)), ((), ())), preferred_element_type=jnp.float32
    )


INTERPRET = False
NORM_ROWS = 16


def gelu(argument):
    return 0.5 * argument * (1.0 + lax.erf(argument * 0.7071067811865476))


def block_columns(rows_ref, gain_ref, taps_hbm, out_hbm, taps_ref, out_ref, hidden_ref, sems, put):
    taps_copy = pltpu.make_async_copy(taps_hbm, taps_ref, sems.at[0])
    out_copy = pltpu.make_async_copy(out_hbm, out_ref, sems.at[1])
    taps_copy.start()
    out_copy.start()
    padded, channels = rows_ref.shape
    count = padded - 2 * DILATION_STEP
    width = out_ref.shape[0]

    def normalize_some(i, carry):
        some = pl.ds(pl.multiple_of(i * NORM_ROWS, NORM_ROWS), NORM_ROWS)
        value = wide(rows_ref[some, :])
        inverse = lax.rsqrt(jnp.mean(value * value, axis=-1, keepdims=True) + 1e-06)
        hidden_ref[some, :] = narrow(gelu(value * inverse * gain_ref[...]))
        return carry

    lax.fori_loop(0, padded // NORM_ROWS, normalize_some, 0, unroll=2)
    taps_copy.wait()
    block = min(256, width)
    for j in range(0, width, block):
        total = jnp.zeros((count, block), jnp.float32)
        for tap in range(3):
            total += dot(
                hidden_ref[tap * DILATION_STEP : tap * DILATION_STEP + count, :],
                taps_ref[tap, :, j : j + block],
            )
        put(slice(j, j + block), total)
    out_copy.wait()
    for j in range(0, channels, block):
        cut = slice(j, j + block)
        yield cut, wide(rows_ref[DILATION_STEP : DILATION_STEP + count, cut]), out_ref[:, cut]


def forward_kernel(
    base_ref, rows_ref, gain_ref, entry_ref, taps_hbm, out_hbm,
    kept_ref, sent_ref, active_ref, block_hbm, sum_hbm,
    taps_ref, out_ref, hidden_ref, pick_ref, block_ref, sum_ref, sems,
):
    count, channels = block_ref.shape
    sum_copy = pltpu.make_async_copy(sum_ref, sum_hbm, sems.at[2])
    block_copy = pltpu.make_async_copy(block_ref, block_hbm, sems.at[3])
    entries = entry_ref.shape[1]
    half = entries // 2
    row = base_ref[0] + lax.broadcasted_iota(jnp.int32, (count, entries), 0)
    pick_ref[...] = narrow(jnp.where(entry_ref[...] == row, 1.0, 0.0))
    core = base_ref[1]
    own = pick_ref.at[:, pl.ds(pl.multiple_of(core * half, half), half)]
    other = pick_ref.at[:, pl.ds(pl.multiple_of((1 - core) * half, half), half)]

    def put(cut, total):
        sum_ref[:, cut] = total
        active_ref[:, cut] = narrow(gelu(total))

    for cut, features, weight in block_columns(
        rows_ref, gain_ref, taps_hbm, out_hbm, taps_ref, out_ref, hidden_ref, sems, put
    ):
        if cut.start == 0:
            sum_copy.start()
        part = narrow(features + dot(active_ref[...], weight))
        block_ref[:, cut] = part
        sent_ref[:, cut] = narrow(dot(other[...], part, (0, 0)))
        kept_ref[:, cut] = narrow(dot(own[...], part, (0, 0)))
    block_copy.start()
    sent_ref[:, channels:] = narrow(dot(other[...], active_ref[...], (0, 0)))
    kept_ref[:, channels:] = narrow(dot(own[...], active_ref[...], (0, 0)))
    sum_copy.wait()
    block_copy.wait()


def reflect_kernel(
    rows_ref, gain_ref, own_ref, perm_ref, taps_hbm, out_hbm, wide_ref, narrow_ref,
    taps_ref, out_ref, hidden_ref, active_ref, partner_ref, mirror_ref, sems,
):
    count, channels = own_ref.shape

    def put(cut, total):
        active_ref[:, cut] = narrow(gelu(total))

    for cut, features, weight in block_columns(
        rows_ref, gain_ref, taps_hbm, out_hbm, taps_ref, out_ref, hidden_ref, sems, put
    ):
        partner_ref[:, cut] = narrow(features + dot(active_ref[...], weight))
    place = lax.broadcasted_iota(jnp.int32, (count, count), 0)
    other = lax.broadcasted_iota(jnp.int32, (count, count), 1)
    reversal = narrow(jnp.where(place + other == count - 1, 1.0, 0.0))
    mirror_ref[...] = narrow(dot(reversal, partner_ref[...]))
    wide_ref[...] = wide(own_ref[...])
    some = min(256, channels)
    for j in range(0, channels, some):
        channel = j + lax.broadcasted_iota(jnp.int32, (some, channels), 0)
        chosen = narrow(jnp.where(perm_ref[...] == channel, 1.0, 0.0))
        wide_ref[...] -= 0.5 * dot(mirror_ref[:, j : j + some], chosen)
        wide_ref[:, j : j + some] -= 0.5 * dot(mirror_ref[...], chosen, (1, 1))
    narrow_ref[...] = narrow(wide_ref[...])


def reflect(padded, norm_gain, block_out, rc_perm, taps, out_weight):
    count, channels = block_out.shape
    vmem = pl.BlockSpec(memory_space=pltpu.VMEM)
    bf = jnp.bfloat16
    return pl.pallas_call(
        reflect_kernel,
        out_shape=[
            jax.ShapeDtypeStruct((count, channels), jnp.float32),
            jax.ShapeDtypeStruct((count, channels), bf),
        ],
        in_specs=[vmem] * 4 + [pl.BlockSpec(memory_space=pltpu.HBM)] * 2,
        out_specs=[vmem] * 2,
        scratch_shapes=[
            pltpu.VMEM(taps.shape, bf),
            pltpu.VMEM(out_weight.shape, bf),
            pltpu.VMEM(padded.shape, bf),
            pltpu.VMEM((count, out_weight.shape[0]), bf),
            pltpu.VMEM((count, channels), bf),
            pltpu.VMEM((count, channels), bf),
            pltpu.SemaphoreType.DMA((2,)),
        ],
        compiler_params=pltpu.CompilerParams(vmem_limit_bytes=20 << 20),
        cost_estimate=pl.CostEstimate(
            flops=count * channels * (8 * out_weight.shape[0] + 4 * channels),
            transcendentals=count * channels,
            bytes_accessed=2 * (taps.size + out_weight.size) + 10 * count * channels,
        ),
        name="reflect",
        interpret=INTERPRET,
    )(
        padded,
        norm_gain[None, :],
        block_out,
        rc_perm[None, :],
        in_hbm(taps),
        in_hbm(out_weight),
    )


def hbm(shape, kind):
    return jax.ShapeDtypeStruct(shape, kind) if INTERPRET else pltpu.HBM(shape, kind)


def in_hbm(value):
    return value if INTERPRET else pltpu.with_memory_space_constraint(value, pltpu.HBM)


def forward(padded, norm_gain, entry_bins, base, taps, out_weight):
    padded_rows, channels = padded.shape
    count = padded_rows - 2 * DILATION_STEP
    width = out_weight.shape[0]
    entries = entry_bins.shape[0]
    vmem = pl.BlockSpec(memory_space=pltpu.VMEM)
    bf = jnp.bfloat16
    payload = jax.ShapeDtypeStruct((entries // 2, channels + width), bf)
    return pl.pallas_call(
        forward_kernel,
        out_shape=[
            payload,
            payload,
            jax.ShapeDtypeStruct((count, width), bf),
            hbm((count, channels), bf),
            hbm((count, width), jnp.float32),
        ],
        in_specs=[pl.BlockSpec(memory_space=pltpu.SMEM), vmem, vmem, vmem]
        + [pl.BlockSpec(memory_space=pltpu.HBM)] * 2,
        out_specs=[vmem] * 3 + [pl.BlockSpec(memory_space=pltpu.HBM)] * 2,
        scratch_shapes=[
            pltpu.VMEM(taps.shape, bf),
            pltpu.VMEM(out_weight.shape, bf),
            pltpu.VMEM((padded_rows, channels), bf),
            pltpu.VMEM((count, entries), bf),
            pltpu.VMEM((count, channels), bf),
            pltpu.VMEM((count, width), jnp.float32),
            pltpu.SemaphoreType.DMA((4,)),
        ],
        compiler_params=pltpu.CompilerParams(vmem_limit_bytes=20 << 20),
        cost_estimate=pl.CostEstimate(
            flops=2 * count * (4 * channels * width + entries * (channels + width)),
            transcendentals=count * (channels + width),
            bytes_accessed=2 * (taps.size + out_weight.size) + 8 * count * channels,
        ),
        name="forward",
        interpret=INTERPRET,
    )(
        base,
        padded,
        norm_gain[None, :],
        entry_bins[None, :],
        in_hbm(taps),
        in_hbm(out_weight),
    )


def after(value, token):
    return lax.optimization_barrier((value, token))[0]


def gather_head(head_weight):
    core = lax.axis_index("core")
    half = head_weight.shape[1] // 2
    mine = jnp.where(core == 0, head_weight[:, :half], head_weight[:, half:]).T
    pieces = [shifted(mine, "x", k) for k in range(1, lax.axis_size("x"))]
    held = jnp.concatenate([mine] + pieces, axis=0)
    return held, shifted(held, "core", 1)


def deal_targets(gene_target, own_strand, own_count):
    nx, nz = lax.axis_size("x"), lax.axis_size("zl")
    x, zl, core = (lax.axis_index(a) for a in ("x", "zl", "core"))
    genes, tracks = gene_target.shape
    odd = (lax.broadcasted_iota(jnp.int32, gene_target.shape, 1) & 1) == 1
    swapped = jnp.where(odd, jnp.roll(gene_target, 1, axis=1), jnp.roll(gene_target, -1, axis=1))
    flipped = jnp.where(own_strand[:, None] == 1, swapped, gene_target)
    parts = flipped.reshape(genes, nx, nz, 2, tracks // (nx * nz * 2))
    parts = jnp.transpose(parts, (1, 2, 0, 3, 4))
    parts = jnp.where(core == 0, parts, parts[:, :, :, ::-1])
    parts = jnp.stack([pick(parts, (x - k) % nx) for k in range(nx)], axis=3)
    parts = parts.reshape(nz, genes, tracks // nz)
    counts = jnp.broadcast_to(wide(own_count)[None, :, None], (nz, genes, 128))
    parts = jnp.concatenate([parts, counts], axis=2)
    pieces = [pick(parts, zl)]
    for k in range(1, nz):
        pieces.append(shifted(pick(parts, (zl + k) % nz), "zl", k))
    return jnp.concatenate(pieces, axis=0)


def listed_bins(exon_bins, exon_count):
    place = lax.broadcasted_iota(jnp.int32, exon_bins.shape, 1)
    return jnp.where(place < exon_count[:, None], exon_bins, -1)


def by_owner(entry_bins):
    ny, nh, nc = (lax.axis_size(a) for a in BINS)
    return entry_bins.reshape(ny, nh, nc, -1).transpose(2, 0, 1, 3).reshape(-1)


def by_distance(entry_bins):
    ny, nh, nc = (lax.axis_size(a) for a in BINS)
    y, zh, core = (lax.axis_index(a) for a in BINS)
    devices = ny * nh * nc
    owner = lax.iota(jnp.int32, devices)
    owner_core = (core + owner // (ny * nh)) % nc
    owner_y = (y + (owner // nh) % ny) % ny
    owner_zh = (zh + owner % nh) % nh
    owner = (owner_y * nh + owner_zh) * nc + owner_core
    entry_bins = entry_bins.reshape(devices, -1)
    chosen = owner[:, None] == lax.iota(jnp.int32, devices)[None, :]
    return jnp.sum(jnp.where(chosen[:, :, None], entry_bins[None], 0), axis=1).reshape(-1)


def whole_step(
    features,
    norm_gain,
    convolution_taps_weight,
    out_weight,
    head_weight,
    rc_perm,
    exon_bins,
    exon_count,
    gene_strand,
    gene_target,
):
    ny, nh, nc, nx, nz = (lax.axis_size(a) for a in ("y", "zh", "core", "x", "zl"))
    y, zh, core, x, zl = (lax.axis_index(a) for a in ("y", "zh", "core", "x", "zl"))
    bin_devices = ny * nh * nc
    bin_index = (y * nh + zh) * nc + core
    rows = features[0]
    count_of_rows, channels = rows.shape
    low, high = edge_rows(rows, DILATION_STEP)
    head, head_other = gather_head(head_weight)
    entry_bins = listed_bins(exon_bins[0], exon_count[0])
    entries = entry_bins.size
    padded_rows = jnp.concatenate([low, rows, high], axis=0)
    partner = lax.ppermute(
        padded_rows, BINS, [(i, bin_devices - 1 - i) for i in range(bin_devices)]
    )
    kept, sent, active, block_out, convolved_sum = forward(
        padded_rows,
        norm_gain,
        by_owner(entry_bins),
        jnp.stack([bin_index * count_of_rows, core]),
        convolution_taps_weight,
        out_weight,
    )

    sent = shifted(sent, "core", 1)
    sent = narrow(wide(kept) + wide(sent)).reshape(ny, -1, kept.shape[1])
    pieces = [shifted(pick(sent, (y + k) % ny), "y", k) for k in range(1, ny)]
    sent = narrow(wide(pick(sent, y)) + sum(wide(piece) for piece in pieces))
    sent = sent.reshape(nh, -1, kept.shape[1])
    piece = shifted(pick(sent, 1 - zh), "zh", 1)
    sent = narrow(wide(pick(sent, zh)) + wide(piece))
    gathered = jnp.concatenate([sent] + [shifted(sent, "zl", k) for k in range(1, nz)], axis=0)
    gathered_active = gathered[:, channels:]
    gathered = gathered[:, :channels]

    distant_bins = by_distance(after(entry_bins, block_out))
    positions = bin_index * count_of_rows + lax.iota(jnp.int32, count_of_rows)
    pick_rows = narrow(distant_bins[None, :] == positions[:, None])
    own_genes = exon_bins.shape[1] // bin_devices
    gene_strand, exon_count = after((gene_strand, exon_count), block_out)
    own_strand = lax.dynamic_slice_in_dim(gene_strand[0], bin_index * own_genes, own_genes, 0)
    own_count = lax.dynamic_slice_in_dim(exon_count[0], bin_index * own_genes, own_genes, 0)
    targets = deal_targets(after(gene_target[0], block_out), own_strand, own_count)
    rc_grad, rc_narrow = reflect(
        partner,
        norm_gain,
        block_out,
        rc_perm,
        convolution_taps_weight,
        out_weight,
    )

    logits = jnp.concatenate([dot(gathered, head, (1, 1)), dot(gathered, head_other, (1, 1))], axis=1)
    grouped = (nz * own_genes, exon_bins.shape[2], logits.shape[1])
    tracks = logits.shape[1]
    predicted = narrow(jax.nn.softplus(logits)).reshape(grouped)
    counted = lax.broadcasted_iota(jnp.int32, grouped[:2], 1) < targets[:, tracks:tracks + 1].astype(
        jnp.int32
    )
    coverage = jnp.sum(jnp.where(counted[:, :, None], wide(predicted), 0.0), axis=1)
    spread_back = narrow(1.0 - targets[:, :tracks] / (1.0 + coverage))
    logit_grad = narrow(
        wide(spread_back)[:, None, :] * jax.nn.sigmoid(logits).reshape(grouped)
    ).reshape(logits.shape)
    entry_grad = narrow(
        dot(logit_grad[:, : tracks // 2], head) + dot(logit_grad[:, tracks // 2 :], head_other)
    )
    back = entry_grad.reshape(nz, -1, channels)
    pieces = [shifted(back[k], "zl", -k) for k in range(1, nz)]
    back = narrow(wide(back[0]) + sum(wide(piece) for piece in pieces))
    back = jnp.concatenate([back, shifted(back, "zh", 1)], axis=0)
    back = jnp.concatenate([back] + [shifted(back, "y", -k) for k in range(1, ny)], axis=0)
    back_other = shifted(back, "core", 1)
    head_back = dot(pick_rows[:, : entries // 2], back) + dot(
        pick_rows[:, entries // 2 :], back_other
    )
    block_grad = narrow(head_back + rc_grad)

    half = channels // 2

    def turn(value):
        return jnp.where(core == 0, value, jnp.roll(value, half, axis=1))

    turned, turned_entries = turn(rc_narrow), turn(entry_grad)

    def share_of(cut):
        return dot(active, turned[:, cut], (0, 0)) + dot(
            gathered_active, turned_entries[:, cut], (0, 0)
        )

    piece = shifted(narrow(share_of(slice(half, None))), "core", 1)
    share = narrow(share_of(slice(0, half)) + wide(piece)).reshape(nx, -1, half)
    pieces = [shifted(pick(share, (x + k) % nx), "x", k) for k in range(1, nx)]
    share = wide(pick(share, x)) + sum(wide(piece) for piece in pieces)
    share = narrow(share).reshape(nz, -1, half)
    pieces = [shifted(pick(share, (zl + k) % nz), "zl", k) for k in range(1, nz)]
    share = narrow(wide(pick(share, zl)) + sum(wide(piece) for piece in pieces))
    share = narrow(
        (wide(share) + wide(shifted(share, "y", 2)))
        + (wide(shifted(share, "y", 1)) + wide(shifted(share, "y", 3)))
    )
    share = wide(share) + wide(shifted(share, "zh", 1))
    other = shifted(share, "core", 1)
    out_weight_grad = jnp.concatenate(
        [jnp.where(core == 0, share, other), jnp.where(core == 0, other, share)], axis=1
    )

    activation_gradient = narrow(dot(block_grad, out_weight, (1, 1)) * gelu_slope(convolved_sum))
    low, high = edge_rows(activation_gradient, DILATION_STEP)
    padded_gradient = jnp.concatenate([low, activation_gradient, high], axis=0)
    hidden_grad = jnp.zeros((count_of_rows, channels), jnp.float32)
    for tap in range(3):
        start = (2 - tap) * DILATION_STEP
        hidden_grad = hidden_grad + dot(
            padded_gradient[start : start + count_of_rows], convolution_taps_weight[tap], (1, 1)
        )
    widened = wide(after(rows, block_out))
    inverse = lax.rsqrt(jnp.mean(widened * widened, axis=-1, keepdims=True) + 1e-06)
    normed = widened * inverse * norm_gain
    normed_grad = hidden_grad * gelu_slope(normed) * norm_gain
    norm_back = inverse * normed_grad - widened * inverse**3 * jnp.mean(
        normed_grad * widened, axis=-1, keepdims=True
    )
    input_grad = narrow(wide(block_grad) + norm_back)
    return (input_grad[None], out_weight_grad)


def solution(mesh):
    cut = Mesh(mesh.devices.reshape(4, 2, 2, 4, 4), BINS + ("x", "zl"))
    batch = ("x", "zl")
    in_specs = (
        P(batch, BINS, None),
        P(),
        P(),
        P(),
        P(None, batch),
        P(),
        P(batch, None, None),
        P(batch, None),
        P(batch, None),
        P(batch, BINS, None),
    )
    out_specs = (P(batch, BINS, None), P(batch, None))
    return jax.shard_map(
        whole_step, mesh=cut, in_specs=in_specs, out_specs=out_specs, check_vma=False
    )
```

```python
import jax
import jax.numpy as jnp
from jax import lax
from jax.experimental import pallas as pl
from jax.experimental.pallas import tpu as pltpu
from jax.sharding import Mesh
from jax.sharding import PartitionSpec as P

DILATION_STEP = 16
BINS = ("y", "zh", "core")


def shifted(block, axis, shift):
    count = lax.axis_size(axis)
    return lax.ppermute(block, axis, [(i, (i + shift) % count) for i in range(count)])


def edge_rows(block, width):
    count = lax.axis_size(BINS)
    low = lax.ppermute(block[-width:], BINS, [(i, i + 1) for i in range(count - 1)])
    high = lax.ppermute(block[:width], BINS, [(i + 1, i) for i in range(count - 1)])
    return low, high


def pick(stack, index):
    return lax.dynamic_index_in_dim(stack, index, 0, keepdims=False)


def wide(value):
    return value.astype(jnp.float32)


def narrow(value):
    return value.astype(jnp.bfloat16)


def gelu_slope(argument):
    return (
        0.5 * (1.0 + jax.scipy.special.erf(argument * 0.7071067811865476))
        + argument * jnp.exp(-0.5 * argument * argument) * 0.3989422804014327
    )


def dot(left, right, over=(1, 0)):
    return lax.dot_general(
        left, right, (((over[0],), (over[1],)), ((), ())), preferred_element_type=jnp.float32
    )


INTERPRET = False
NORM_ROWS = 16


def gelu(argument):
    return 0.5 * argument * (1.0 + lax.erf(argument * 0.7071067811865476))


def block_columns(
    edge_ref, rows_ref, gain_ref, taps_hbm, out_hbm, taps_ref, out_ref, hidden_ref, active_ref,
    sems, put, emit, before_emit=None,
):
    taps_copy = pltpu.make_async_copy(taps_hbm, taps_ref, sems.at[0])
    out_copy = pltpu.make_async_copy(out_hbm, out_ref, sems.at[1])
    taps_copy.start()
    out_copy.start()
    count, channels = rows_ref.shape
    width = out_ref.shape[0]

    def normalize_some(value):
        value = wide(value)
        inverse = lax.rsqrt(jnp.mean(value * value, axis=-1, keepdims=True) + 1e-06)
        return narrow(gelu(value * inverse * gain_ref[...]))

    def normalize_rows(i, carry):
        start = pl.multiple_of(i * NORM_ROWS, NORM_ROWS)
        hidden_ref[pl.ds(start + DILATION_STEP, NORM_ROWS), :] = normalize_some(
            rows_ref[pl.ds(start, NORM_ROWS), :]
        )
        return carry

    hidden_ref[:DILATION_STEP, :] = normalize_some(edge_ref[:DILATION_STEP, :])
    hidden_ref[DILATION_STEP + count :, :] = normalize_some(edge_ref[DILATION_STEP:, :])
    lax.fori_loop(0, count // NORM_ROWS, normalize_rows, 0, unroll=2)
    taps_copy.wait()
    block = min(256, width)

    def columns(j):
        return pl.ds(pl.multiple_of(j * block, block), block)

    def convolve(j, carry):
        cut = columns(j)
        total = jnp.zeros((count, block), jnp.float32)
        for tap in range(3):
            total += dot(
                hidden_ref[tap * DILATION_STEP : tap * DILATION_STEP + count, :],
                taps_ref[tap, :, cut],
            )
        put(cut, total)
        return carry

    lax.fori_loop(0, width // block, convolve, 0)
    out_copy.wait()

    def project(j, carry):
        cut = columns(j)
        emit(cut, narrow(wide(rows_ref[:, cut]) + dot(active_ref[...], out_ref[:, cut])))
        return carry

    if before_emit:
        before_emit()
    lax.fori_loop(0, channels // block, project, 0)


def forward_kernel(
    base_ref, edge_ref, rows_ref, gain_ref, entry_ref, taps_hbm, out_hbm,
    kept_ref, sent_ref, active_ref, block_hbm, sum_hbm,
    taps_ref, out_ref, hidden_ref, pick_ref, block_ref, sum_ref, sems,
):
    count, channels = block_ref.shape
    sum_copy = pltpu.make_async_copy(sum_ref, sum_hbm, sems.at[2])
    block_copy = pltpu.make_async_copy(block_ref, block_hbm, sems.at[3])
    entries = entry_ref.shape[1]
    half = entries // 2
    row = base_ref[0] + lax.broadcasted_iota(jnp.int32, (count, entries), 0)
    pick_ref[...] = narrow(jnp.where(entry_ref[...] == row, 1.0, 0.0))
    core = base_ref[1]
    own = pick_ref.at[:, pl.ds(pl.multiple_of(core * half, half), half)]
    other = pick_ref.at[:, pl.ds(pl.multiple_of((1 - core) * half, half), half)]

    def put(cut, total):
        sum_ref[:, cut] = total
        active_ref[:, cut] = narrow(gelu(total))

    def emit(cut, part):
        block_ref[:, cut] = part
        sent_ref[:, cut] = narrow(dot(other[...], part, (0, 0)))
        kept_ref[:, cut] = narrow(dot(own[...], part, (0, 0)))

    block_columns(
        edge_ref, rows_ref, gain_ref, taps_hbm, out_hbm, taps_ref, out_ref, hidden_ref, active_ref,
        sems, put, emit, sum_copy.start,
    )
    block_copy.start()
    sent_ref[:, channels:] = narrow(dot(other[...], active_ref[...], (0, 0)))
    kept_ref[:, channels:] = narrow(dot(own[...], active_ref[...], (0, 0)))
    sum_copy.wait()
    block_copy.wait()


def reflect_kernel(
    padded_ref, gain_ref, own_ref, perm_ref, taps_hbm, out_hbm, wide_ref, narrow_ref,
    taps_ref, out_ref, hidden_ref, active_ref, partner_ref, mirror_ref, sems,
):
    count, channels = own_ref.shape
    edge_ref = padded_ref.at[: 2 * DILATION_STEP, :]
    rows_ref = padded_ref.at[2 * DILATION_STEP :, :]

    def put(cut, total):
        active_ref[:, cut] = narrow(gelu(total))

    def emit(cut, part):
        partner_ref[:, cut] = part

    block_columns(
        edge_ref, rows_ref, gain_ref, taps_hbm, out_hbm, taps_ref, out_ref, hidden_ref, active_ref,
        sems, put, emit,
    )
    place = lax.broadcasted_iota(jnp.int32, (count, count), 0)
    other = lax.broadcasted_iota(jnp.int32, (count, count), 1)
    reversal = narrow(jnp.where(place + other == count - 1, 1.0, 0.0))
    mirror_ref[...] = narrow(dot(reversal, partner_ref[...]))
    wide_ref[...] = wide(own_ref[...])
    some = min(256, channels)

    def mix(j, carry):
        cut = pl.ds(pl.multiple_of(j * some, some), some)
        channel = j * some + lax.broadcasted_iota(jnp.int32, (some, channels), 0)
        chosen = narrow(jnp.where(perm_ref[...] == channel, 1.0, 0.0))
        wide_ref[...] -= 0.5 * dot(mirror_ref[:, cut], chosen)
        wide_ref[:, cut] -= 0.5 * dot(mirror_ref[...], chosen, (1, 1))
        return carry

    lax.fori_loop(0, channels // some, mix, 0)
    narrow_ref[...] = narrow(wide_ref[...])


def reflect(padded, norm_gain, block_out, rc_perm, taps, out_weight):
    count, channels = block_out.shape
    vmem = pl.BlockSpec(memory_space=pltpu.VMEM)
    bf = jnp.bfloat16
    return pl.pallas_call(
        reflect_kernel,
        out_shape=[
            jax.ShapeDtypeStruct((count, channels), jnp.float32),
            jax.ShapeDtypeStruct((count, channels), bf),
        ],
        in_specs=[vmem] * 4 + [pl.BlockSpec(memory_space=pltpu.HBM)] * 2,
        out_specs=[vmem] * 2,
        scratch_shapes=[
            pltpu.VMEM(taps.shape, bf),
            pltpu.VMEM(out_weight.shape, bf),
            pltpu.VMEM((count + 2 * DILATION_STEP, channels), bf),
            pltpu.VMEM((count, out_weight.shape[0]), bf),
            pltpu.VMEM((count, channels), bf),
            pltpu.VMEM((count, channels), bf),
            pltpu.SemaphoreType.DMA((2,)),
        ],
        compiler_params=pltpu.CompilerParams(vmem_limit_bytes=20 << 20),
        cost_estimate=pl.CostEstimate(
            flops=count * channels * (8 * out_weight.shape[0] + 4 * channels),
            transcendentals=count * channels,
            bytes_accessed=2 * (taps.size + out_weight.size) + 10 * count * channels,
        ),
        name="reflect",
        interpret=INTERPRET,
    )(
        padded,
        norm_gain[None, :],
        block_out,
        rc_perm[None, :],
        in_hbm(taps),
        in_hbm(out_weight),
    )


def hbm(shape, kind):
    return jax.ShapeDtypeStruct(shape, kind) if INTERPRET else pltpu.HBM(shape, kind)


def in_hbm(value):
    return value if INTERPRET else pltpu.with_memory_space_constraint(value, pltpu.HBM)


def forward(edges, rows, norm_gain, entry_bins, base, taps, out_weight):
    count, channels = rows.shape
    width = out_weight.shape[0]
    entries = entry_bins.shape[0]
    vmem = pl.BlockSpec(memory_space=pltpu.VMEM)
    bf = jnp.bfloat16
    payload = jax.ShapeDtypeStruct((entries // 2, channels + width), bf)
    return pl.pallas_call(
        forward_kernel,
        out_shape=[
            payload,
            payload,
            jax.ShapeDtypeStruct((count, width), bf),
            hbm((count, channels), bf),
            hbm((count, width), jnp.float32),
        ],
        in_specs=[pl.BlockSpec(memory_space=pltpu.SMEM), vmem, vmem, vmem, vmem]
        + [pl.BlockSpec(memory_space=pltpu.HBM)] * 2,
        out_specs=[vmem] * 3 + [pl.BlockSpec(memory_space=pltpu.HBM)] * 2,
        scratch_shapes=[
            pltpu.VMEM(taps.shape, bf),
            pltpu.VMEM(out_weight.shape, bf),
            pltpu.VMEM((count + 2 * DILATION_STEP, channels), bf),
            pltpu.VMEM((count, entries), bf),
            pltpu.VMEM((count, channels), bf),
            pltpu.VMEM((count, width), jnp.float32),
            pltpu.SemaphoreType.DMA((4,)),
        ],
        compiler_params=pltpu.CompilerParams(vmem_limit_bytes=20 << 20),
        cost_estimate=pl.CostEstimate(
            flops=2 * count * (4 * channels * width + entries * (channels + width)),
            transcendentals=count * (channels + width),
            bytes_accessed=2 * (taps.size + out_weight.size) + 8 * count * channels,
        ),
        name="forward",
        interpret=INTERPRET,
    )(
        base,
        edges,
        rows,
        norm_gain[None, :],
        entry_bins[None, :],
        in_hbm(taps),
        in_hbm(out_weight),
    )


def after(value, token):
    return lax.optimization_barrier((value, token))[0]


def gather_head(head_weight):
    core = lax.axis_index("core")
    half = head_weight.shape[1] // 2
    mine = jnp.where(core == 0, head_weight[:, :half], head_weight[:, half:]).T
    pieces = [shifted(mine, "x", k) for k in range(1, lax.axis_size("x"))]
    held = jnp.concatenate([mine] + pieces, axis=0)
    return held, shifted(held, "core", 1)


def deal_targets(gene_target, own_strand, own_count):
    nx, nz = lax.axis_size("x"), lax.axis_size("zl")
    x, zl, core = (lax.axis_index(a) for a in ("x", "zl", "core"))
    genes, tracks = gene_target.shape
    odd = (lax.broadcasted_iota(jnp.int32, gene_target.shape, 1) & 1) == 1
    swapped = jnp.where(odd, jnp.roll(gene_target, 1, axis=1), jnp.roll(gene_target, -1, axis=1))
    flipped = jnp.where(own_strand[:, None] == 1, swapped, gene_target)
    parts = flipped.reshape(genes, nx, nz, 2, tracks // (nx * nz * 2))
    parts = jnp.transpose(parts, (1, 2, 0, 3, 4))
    parts = jnp.where(core == 0, parts, parts[:, :, :, ::-1])
    parts = jnp.stack([pick(parts, (x - k) % nx) for k in range(nx)], axis=3)
    parts = parts.reshape(nz, genes, tracks // nz)
    counts = jnp.broadcast_to(wide(own_count)[None, :, None], (nz, genes, 128))
    parts = jnp.concatenate([parts, counts], axis=2)
    parts = lax.all_to_all(parts, "zl", split_axis=0, concat_axis=0, tiled=True)
    return jnp.concatenate([pick(parts, (zl - k) % nz) for k in range(nz)], axis=0)


def listed_bins(exon_bins, exon_count):
    place = lax.broadcasted_iota(jnp.int32, exon_bins.shape, 1)
    return jnp.where(place < exon_count[:, None], exon_bins, -1)


def by_owner(entry_bins):
    ny, nh, nc = (lax.axis_size(a) for a in BINS)
    return entry_bins.reshape(ny, nh, nc, -1).transpose(2, 0, 1, 3).reshape(-1)


def by_distance(entry_bins):
    ny, nh, nc = (lax.axis_size(a) for a in BINS)
    y, zh, core = (lax.axis_index(a) for a in BINS)
    devices = ny * nh * nc
    owner = lax.iota(jnp.int32, devices)
    owner_core = (core + owner // (ny * nh)) % nc
    owner_y = (y + (owner // nh) % ny) % ny
    owner_zh = (zh + owner % nh) % nh
    owner = (owner_y * nh + owner_zh) * nc + owner_core
    entry_bins = entry_bins.reshape(devices, -1)
    chosen = owner[:, None] == lax.iota(jnp.int32, devices)[None, :]
    return jnp.sum(jnp.where(chosen[:, :, None], entry_bins[None], 0), axis=1).reshape(-1)


def whole_step(
    features,
    norm_gain,
    convolution_taps_weight,
    out_weight,
    head_weight,
    rc_perm,
    exon_bins,
    exon_count,
    gene_strand,
    gene_target,
):
    ny, nh, nc, nx, nz = (lax.axis_size(a) for a in ("y", "zh", "core", "x", "zl"))
    y, zh, core, x, _ = (lax.axis_index(a) for a in ("y", "zh", "core", "x", "zl"))
    bin_devices = ny * nh * nc
    bin_index = (y * nh + zh) * nc + core
    rows = features[0]
    count_of_rows, channels = rows.shape
    low, high = edge_rows(rows, DILATION_STEP)
    head, head_other = gather_head(head_weight)
    entry_bins = listed_bins(exon_bins[0], exon_count[0])
    entries = entry_bins.size
    edges = jnp.concatenate([low, high], axis=0)
    partner = lax.ppermute(
        jnp.concatenate([edges, rows], axis=0),
        BINS,
        [(i, bin_devices - 1 - i) for i in range(bin_devices)],
    )
    kept, sent, active, block_out, convolved_sum = forward(
        edges,
        rows,
        norm_gain,
        by_owner(entry_bins),
        jnp.stack([bin_index * count_of_rows, core]),
        convolution_taps_weight,
        out_weight,
    )

    sent = shifted(sent, "core", 1)
    sent = narrow(wide(kept) + wide(sent)).reshape(ny, -1, kept.shape[1])
    pieces = [shifted(pick(sent, (y + k) % ny), "y", k) for k in range(1, ny)]
    sent = narrow(wide(pick(sent, y)) + sum(wide(piece) for piece in pieces))
    sent = sent.reshape(nh, -1, kept.shape[1])
    piece = shifted(pick(sent, 1 - zh), "zh", 1)
    sent = narrow(wide(pick(sent, zh)) + wide(piece))
    gathered = jnp.concatenate([sent] + [shifted(sent, "zl", k) for k in range(1, nz)], axis=0)
    gathered_active = gathered[:, channels:]
    gathered = gathered[:, :channels]

    distant_bins = by_distance(after(entry_bins, block_out))
    positions = bin_index * count_of_rows + lax.iota(jnp.int32, count_of_rows)
    pick_rows = narrow(distant_bins[None, :] == positions[:, None])
    own_genes = exon_bins.shape[1] // bin_devices
    gene_strand, exon_count = after((gene_strand, exon_count), block_out)
    own_strand = lax.dynamic_slice_in_dim(gene_strand[0], bin_index * own_genes, own_genes, 0)
    own_count = lax.dynamic_slice_in_dim(exon_count[0], bin_index * own_genes, own_genes, 0)
    targets = deal_targets(after(gene_target[0], block_out), own_strand, own_count)
    rc_grad, rc_narrow = reflect(
        partner,
        norm_gain,
        block_out,
        rc_perm,
        convolution_taps_weight,
        out_weight,
    )

    logits = jnp.concatenate([dot(gathered, head, (1, 1)), dot(gathered, head_other, (1, 1))], axis=1)
    grouped = (nz * own_genes, exon_bins.shape[2], logits.shape[1])
    tracks = logits.shape[1]
    predicted = narrow(jax.nn.softplus(logits)).reshape(grouped)
    counted = lax.broadcasted_iota(jnp.int32, grouped[:2], 1) < targets[:, tracks:tracks + 1].astype(
        jnp.int32
    )
    coverage = jnp.sum(jnp.where(counted[:, :, None], wide(predicted), 0.0), axis=1)
    spread_back = narrow(1.0 - targets[:, :tracks] / (1.0 + coverage))
    logit_grad = narrow(
        wide(spread_back)[:, None, :] * jax.nn.sigmoid(logits).reshape(grouped)
    ).reshape(logits.shape)
    entry_grad = narrow(
        dot(logit_grad[:, : tracks // 2], head) + dot(logit_grad[:, tracks // 2 :], head_other)
    )
    back = entry_grad.reshape(nz, -1, channels)
    pieces = [shifted(back[k], "zl", -k) for k in range(1, nz)]
    back = narrow(wide(back[0]) + sum(wide(piece) for piece in pieces))
    back = jnp.concatenate([back, shifted(back, "zh", 1)], axis=0)
    back = jnp.concatenate([back] + [shifted(back, "y", -k) for k in range(1, ny)], axis=0)
    back_other = shifted(back, "core", 1)
    head_back = dot(pick_rows[:, : entries // 2], back) + dot(
        pick_rows[:, entries // 2 :], back_other
    )
    block_grad = narrow(head_back + rc_grad)

    half = channels // 2

    def turn(value):
        return jnp.where(core == 0, value, jnp.roll(value, half, axis=1))

    turned, turned_entries = turn(rc_narrow), turn(entry_grad)

    def share_of(cut):
        return dot(active, turned[:, cut], (0, 0)) + dot(
            gathered_active, turned_entries[:, cut], (0, 0)
        )

    piece = shifted(narrow(share_of(slice(half, None))), "core", 1)
    share = narrow(share_of(slice(0, half)) + wide(piece)).reshape(nx, -1, half)
    pieces = [shifted(pick(share, (x + k) % nx), "x", k) for k in range(1, nx)]
    share = wide(pick(share, x)) + sum(wide(piece) for piece in pieces)
    share = narrow(share).reshape(nz, -1, half)
    pieces = lax.all_to_all(share, "zl", split_axis=0, concat_axis=0, tiled=True)
    share = narrow(jnp.sum(wide(pieces), axis=0))
    share = narrow(
        (wide(share) + wide(shifted(share, "y", 2)))
        + (wide(shifted(share, "y", 1)) + wide(shifted(share, "y", 3)))
    )
    share = wide(share) + wide(shifted(share, "zh", 1))
    other = shifted(share, "core", 1)
    out_weight_grad = jnp.concatenate(
        [jnp.where(core == 0, share, other), jnp.where(core == 0, other, share)], axis=1
    )

    activation_gradient = narrow(dot(block_grad, out_weight, (1, 1)) * gelu_slope(convolved_sum))
    low, high = edge_rows(activation_gradient, DILATION_STEP)
    padded_gradient = jnp.concatenate([low, activation_gradient, high], axis=0)
    hidden_grad = jnp.zeros((count_of_rows, channels), jnp.float32)
    for tap in range(3):
        start = (2 - tap) * DILATION_STEP
        hidden_grad = hidden_grad + dot(
            padded_gradient[start : start + count_of_rows], convolution_taps_weight[tap], (1, 1)
        )
    widened = wide(after(rows, block_out))
    inverse = lax.rsqrt(jnp.mean(widened * widened, axis=-1, keepdims=True) + 1e-06)
    normed = widened * inverse * norm_gain
    normed_grad = hidden_grad * gelu_slope(normed) * norm_gain
    norm_back = inverse * normed_grad - widened * inverse**3 * jnp.mean(
        normed_grad * widened, axis=-1, keepdims=True
    )
    input_grad = narrow(wide(block_grad) + norm_back)
    return (input_grad[None], out_weight_grad)


def solution(mesh):
    cut = Mesh(mesh.devices.reshape(4, 2, 2, 4, 4), BINS + ("x", "zl"))
    batch = ("x", "zl")
    in_specs = (
        P(batch, BINS, None),
        P(),
        P(),
        P(),
        P(None, batch),
        P(),
        P(batch, None, None),
        P(batch, None),
        P(batch, None),
        P(batch, BINS, None),
    )
    out_specs = (P(batch, BINS, None), P(batch, None))
    return jax.shard_map(
        whole_step, mesh=cut, in_specs=in_specs, out_specs=out_specs, check_vma=False
    )
```

```python
import jax
import jax.numpy as jnp
from jax import lax
from jax.experimental import pallas as pl
from jax.experimental.pallas import tpu as pltpu
from jax.sharding import Mesh
from jax.sharding import PartitionSpec as P

DILATION_STEP = 16
BINS = ("y", "zh", "core")


def shifted(block, axis, shift):
    count = lax.axis_size(axis)
    return lax.ppermute(block, axis, [(i, (i + shift) % count) for i in range(count)])


def edge_rows(block, width):
    count = lax.axis_size(BINS)
    low = lax.ppermute(block[-width:], BINS, [(i, i + 1) for i in range(count - 1)])
    high = lax.ppermute(block[:width], BINS, [(i + 1, i) for i in range(count - 1)])
    return low, high


def pick(stack, index):
    return lax.dynamic_index_in_dim(stack, index, 0, keepdims=False)


def wide(value):
    return value.astype(jnp.float32)


def narrow(value):
    return value.astype(jnp.bfloat16)


def gelu_slope(argument):
    return (
        0.5 * (1.0 + jax.scipy.special.erf(argument * 0.7071067811865476))
        + argument * jnp.exp(-0.5 * argument * argument) * 0.3989422804014327
    )


def dot(left, right, over=(1, 0)):
    return lax.dot_general(
        left, right, (((over[0],), (over[1],)), ((), ())), preferred_element_type=jnp.float32
    )


INTERPRET = False
NORM_ROWS = 16


def gelu(argument):
    return 0.5 * argument * (1.0 + lax.erf(argument * 0.7071067811865476))


def block_columns(
    edge_ref, rows_ref, gain_ref, taps_hbm, out_hbm, taps_ref, out_ref, hidden_ref, active_ref,
    sems, put, emit, before_emit=None,
):
    taps_copy = pltpu.make_async_copy(taps_hbm, taps_ref, sems.at[0])
    out_copy = pltpu.make_async_copy(out_hbm, out_ref, sems.at[1])
    taps_copy.start()
    out_copy.start()
    count, channels = rows_ref.shape
    width = out_ref.shape[0]

    def normalize_some(value):
        value = wide(value)
        inverse = lax.rsqrt(jnp.mean(value * value, axis=-1, keepdims=True) + 1e-06)
        return narrow(gelu(value * inverse * gain_ref[...]))

    def normalize_rows(i, carry):
        start = pl.multiple_of(i * NORM_ROWS, NORM_ROWS)
        hidden_ref[pl.ds(start + DILATION_STEP, NORM_ROWS), :] = normalize_some(
            rows_ref[pl.ds(start, NORM_ROWS), :]
        )
        return carry

    hidden_ref[:DILATION_STEP, :] = normalize_some(edge_ref[:DILATION_STEP, :])
    hidden_ref[DILATION_STEP + count :, :] = normalize_some(edge_ref[DILATION_STEP:, :])
    lax.fori_loop(0, count // NORM_ROWS, normalize_rows, 0, unroll=2)
    taps_copy.wait()
    block = min(256, width)

    def columns(j):
        return pl.ds(pl.multiple_of(j * block, block), block)

    def convolve(j, carry):
        cut = columns(j)
        total = jnp.zeros((count, block), jnp.float32)
        for tap in range(3):
            total += dot(
                hidden_ref[tap * DILATION_STEP : tap * DILATION_STEP + count, :],
                taps_ref[tap, :, cut],
            )
        put(cut, total)
        return carry

    lax.fori_loop(0, width // block, convolve, 0)
    out_copy.wait()

    def project(j, carry):
        cut = columns(j)
        emit(cut, narrow(wide(rows_ref[:, cut]) + dot(active_ref[...], out_ref[:, cut])))
        return carry

    if before_emit:
        before_emit()
    lax.fori_loop(0, channels // block, project, 0)


def forward_kernel(
    base_ref, edge_ref, rows_ref, gain_ref, entry_ref, taps_hbm, out_hbm,
    kept_ref, sent_ref, active_ref, block_hbm, sum_hbm,
    taps_ref, out_ref, hidden_ref, pick_ref, block_ref, sum_ref, sems,
):
    count, channels = block_ref.shape
    sum_copy = pltpu.make_async_copy(sum_ref, sum_hbm, sems.at[2])
    block_copy = pltpu.make_async_copy(block_ref, block_hbm, sems.at[3])
    entries = entry_ref.shape[1]
    half = entries // 2
    row = base_ref[0] + lax.broadcasted_iota(jnp.int32, (count, entries), 0)
    pick_ref[...] = narrow(jnp.where(entry_ref[...] == row, 1.0, 0.0))
    core = base_ref[1]
    own = pick_ref.at[:, pl.ds(pl.multiple_of(core * half, half), half)]
    other = pick_ref.at[:, pl.ds(pl.multiple_of((1 - core) * half, half), half)]

    def put(cut, total):
        sum_ref[:, cut] = total
        active_ref[:, cut] = narrow(gelu(total))

    def emit(cut, part):
        block_ref[:, cut] = part
        sent_ref[:, cut] = narrow(dot(other[...], part, (0, 0)))
        kept_ref[:, cut] = narrow(dot(own[...], part, (0, 0)))

    block_columns(
        edge_ref, rows_ref, gain_ref, taps_hbm, out_hbm, taps_ref, out_ref, hidden_ref, active_ref,
        sems, put, emit, sum_copy.start,
    )
    block_copy.start()
    sent_ref[:, channels:] = narrow(dot(other[...], active_ref[...], (0, 0)))
    kept_ref[:, channels:] = narrow(dot(own[...], active_ref[...], (0, 0)))
    sum_copy.wait()
    block_copy.wait()


def reflect_kernel(
    padded_ref, gain_ref, own_ref, perm_ref, taps_hbm, out_hbm, wide_ref, narrow_ref,
    taps_ref, out_ref, hidden_ref, active_ref, partner_ref, mirror_ref, sems,
):
    count, channels = own_ref.shape
    edge_ref = padded_ref.at[: 2 * DILATION_STEP, :]
    rows_ref = padded_ref.at[2 * DILATION_STEP :, :]

    def put(cut, total):
        active_ref[:, cut] = narrow(gelu(total))

    def emit(cut, part):
        partner_ref[:, cut] = part

    block_columns(
        edge_ref, rows_ref, gain_ref, taps_hbm, out_hbm, taps_ref, out_ref, hidden_ref, active_ref,
        sems, put, emit,
    )
    place = lax.broadcasted_iota(jnp.int32, (count, count), 0)
    other = lax.broadcasted_iota(jnp.int32, (count, count), 1)
    reversal = narrow(jnp.where(place + other == count - 1, 1.0, 0.0))
    mirror_ref[...] = narrow(dot(reversal, partner_ref[...]))
    wide_ref[...] = wide(own_ref[...])
    some = min(256, channels)

    def mix(j, carry):
        cut = pl.ds(pl.multiple_of(j * some, some), some)
        channel = j * some + lax.broadcasted_iota(jnp.int32, (some, channels), 0)
        chosen = narrow(jnp.where(perm_ref[...] == channel, 1.0, 0.0))
        wide_ref[...] -= 0.5 * dot(mirror_ref[:, cut], chosen)
        wide_ref[:, cut] -= 0.5 * dot(mirror_ref[...], chosen, (1, 1))
        return carry

    lax.fori_loop(0, channels // some, mix, 0)
    narrow_ref[...] = narrow(wide_ref[...])


def reflect(padded, norm_gain, block_out, rc_perm, taps, out_weight):
    count, channels = block_out.shape
    vmem = pl.BlockSpec(memory_space=pltpu.VMEM)
    bf = jnp.bfloat16
    return pl.pallas_call(
        reflect_kernel,
        out_shape=[
            jax.ShapeDtypeStruct((count, channels), jnp.float32),
            jax.ShapeDtypeStruct((count, channels), bf),
        ],
        in_specs=[vmem] * 4 + [pl.BlockSpec(memory_space=pltpu.HBM)] * 2,
        out_specs=[vmem] * 2,
        scratch_shapes=[
            pltpu.VMEM(taps.shape, bf),
            pltpu.VMEM(out_weight.shape, bf),
            pltpu.VMEM((count + 2 * DILATION_STEP, channels), bf),
            pltpu.VMEM((count, out_weight.shape[0]), bf),
            pltpu.VMEM((count, channels), bf),
            pltpu.VMEM((count, channels), bf),
            pltpu.SemaphoreType.DMA((2,)),
        ],
        compiler_params=pltpu.CompilerParams(vmem_limit_bytes=20 << 20),
        cost_estimate=pl.CostEstimate(
            flops=count * channels * (8 * out_weight.shape[0] + 4 * channels),
            transcendentals=count * channels,
            bytes_accessed=2 * (taps.size + out_weight.size) + 10 * count * channels,
        ),
        name="reflect",
        interpret=INTERPRET,
    )(
        padded,
        norm_gain[None, :],
        block_out,
        rc_perm[None, :],
        in_hbm(taps),
        in_hbm(out_weight),
    )


def hbm(shape, kind):
    return jax.ShapeDtypeStruct(shape, kind) if INTERPRET else pltpu.HBM(shape, kind)


def in_hbm(value):
    return value if INTERPRET else pltpu.with_memory_space_constraint(value, pltpu.HBM)


def forward(edges, rows, norm_gain, entry_bins, base, taps, out_weight):
    count, channels = rows.shape
    width = out_weight.shape[0]
    entries = entry_bins.shape[0]
    vmem = pl.BlockSpec(memory_space=pltpu.VMEM)
    bf = jnp.bfloat16
    payload = jax.ShapeDtypeStruct((entries // 2, channels + width), bf)
    return pl.pallas_call(
        forward_kernel,
        out_shape=[
            payload,
            payload,
            jax.ShapeDtypeStruct((count, width), bf),
            hbm((count, channels), bf),
            hbm((count, width), jnp.float32),
        ],
        in_specs=[pl.BlockSpec(memory_space=pltpu.SMEM), vmem, vmem, vmem, vmem]
        + [pl.BlockSpec(memory_space=pltpu.HBM)] * 2,
        out_specs=[vmem] * 3 + [pl.BlockSpec(memory_space=pltpu.HBM)] * 2,
        scratch_shapes=[
            pltpu.VMEM(taps.shape, bf),
            pltpu.VMEM(out_weight.shape, bf),
            pltpu.VMEM((count + 2 * DILATION_STEP, channels), bf),
            pltpu.VMEM((count, entries), bf),
            pltpu.VMEM((count, channels), bf),
            pltpu.VMEM((count, width), jnp.float32),
            pltpu.SemaphoreType.DMA((4,)),
        ],
        compiler_params=pltpu.CompilerParams(vmem_limit_bytes=20 << 20),
        cost_estimate=pl.CostEstimate(
            flops=2 * count * (4 * channels * width + entries * (channels + width)),
            transcendentals=count * (channels + width),
            bytes_accessed=2 * (taps.size + out_weight.size) + 8 * count * channels,
        ),
        name="forward",
        interpret=INTERPRET,
    )(
        base,
        edges,
        rows,
        norm_gain[None, :],
        entry_bins[None, :],
        in_hbm(taps),
        in_hbm(out_weight),
    )


def after(value, token):
    return lax.optimization_barrier((value, token))[0]


def gather_head(head_weight):
    mine = head_weight.T
    pieces = [shifted(mine, "x", k) for k in range(1, lax.axis_size("x"))]
    return jnp.concatenate([mine] + pieces, axis=0)


def target_rows(gene_target, own_strand, own_count, columns):
    nx, nz = lax.axis_size("x"), lax.axis_size("zl")
    x = lax.axis_index("x")
    genes, tracks = gene_target.shape
    odd = (lax.broadcasted_iota(jnp.int32, gene_target.shape, 1) & 1) == 1
    swapped = jnp.where(odd, jnp.roll(gene_target, 1, axis=1), jnp.roll(gene_target, -1, axis=1))
    flipped = jnp.where(own_strand[:, None] == 1, swapped, gene_target)
    parts = flipped.reshape(genes, nx, nz, tracks // (nx * nz))
    parts = jnp.transpose(parts, (1, 2, 0, 3))
    parts = jnp.concatenate([pick(parts, (x - k) % nx) for k in range(nx)], axis=2)
    rounded = lax.reduce_precision(parts, 8, 7)
    rest = columns - 2 * parts.shape[2]
    counts = jnp.broadcast_to(wide(own_count)[None, :, None], (nz, genes, rest))
    return narrow(jnp.concatenate([rounded, parts - rounded, counts], axis=2))


def listed_bins(exon_bins, exon_count):
    place = lax.broadcasted_iota(jnp.int32, exon_bins.shape, 1)
    return jnp.where(place < exon_count[:, None], exon_bins, -1)


def by_owner(entry_bins):
    ny, nh, nc = (lax.axis_size(a) for a in BINS)
    return entry_bins.reshape(ny, nh, nc, -1).transpose(2, 0, 1, 3).reshape(-1)


def by_distance(entry_bins):
    ny, nh, nc = (lax.axis_size(a) for a in BINS)
    y, zh, core = (lax.axis_index(a) for a in BINS)
    devices = ny * nh * nc
    owner = lax.iota(jnp.int32, devices)
    owner_core = (core + owner // (ny * nh)) % nc
    owner_y = (y + (owner // nh) % ny) % ny
    owner_zh = (zh + owner % nh) % nh
    owner = (owner_y * nh + owner_zh) * nc + owner_core
    entry_bins = entry_bins.reshape(devices, -1)
    chosen = owner[:, None] == lax.iota(jnp.int32, devices)[None, :]
    return jnp.sum(jnp.where(chosen[:, :, None], entry_bins[None], 0), axis=1).reshape(-1)


def whole_step(
    features,
    norm_gain,
    convolution_taps_weight,
    out_weight,
    head_weight,
    rc_perm,
    exon_bins,
    exon_count,
    gene_strand,
    gene_target,
):
    ny, nh, nc, nx, nz = (lax.axis_size(a) for a in ("y", "zh", "core", "x", "zl"))
    y, zh, core, x, zl = (lax.axis_index(a) for a in ("y", "zh", "core", "x", "zl"))
    bin_devices = ny * nh * nc
    bin_index = (y * nh + zh) * nc + core
    rows = features[0]
    count_of_rows, channels = rows.shape
    low, high = edge_rows(rows, DILATION_STEP)
    head = gather_head(head_weight)
    entry_bins = listed_bins(exon_bins[0], exon_count[0])
    entries = entry_bins.size
    edges = jnp.concatenate([low, high], axis=0)
    partner = lax.ppermute(
        jnp.concatenate([edges, rows], axis=0),
        BINS,
        [(i, bin_devices - 1 - i) for i in range(bin_devices)],
    )
    kept, sent, active, block_out, convolved_sum = forward(
        edges,
        rows,
        norm_gain,
        by_owner(entry_bins),
        jnp.stack([bin_index * count_of_rows, core]),
        convolution_taps_weight,
        out_weight,
    )

    sent = shifted(sent, "core", 1)
    sent = narrow(wide(kept) + wide(sent)).reshape(ny, -1, kept.shape[1])
    pieces = [shifted(pick(sent, (y + k) % ny), "y", k) for k in range(1, ny)]
    sent = narrow(wide(pick(sent, y)) + sum(wide(piece) for piece in pieces))
    sent = sent.reshape(nh, -1, kept.shape[1])
    piece = shifted(pick(sent, 1 - zh), "zh", 1)
    sent = narrow(wide(pick(sent, zh)) + wide(piece))
    distant_bins = by_distance(after(entry_bins, block_out))
    positions = bin_index * count_of_rows + lax.iota(jnp.int32, count_of_rows)
    pick_rows = narrow(distant_bins[None, :] == positions[:, None])
    own_genes = exon_bins.shape[1] // bin_devices
    gene_strand, exon_count = after((gene_strand, exon_count), block_out)
    own_strand = lax.dynamic_slice_in_dim(gene_strand[0], bin_index * own_genes, own_genes, 0)
    own_count = lax.dynamic_slice_in_dim(exon_count[0], bin_index * own_genes, own_genes, 0)
    target = target_rows(
        after(gene_target[0], block_out), own_strand, own_count, kept.shape[1]
    )
    pieces = [jnp.concatenate([sent, pick(target, zl)], axis=0)]
    for k in range(1, nz):
        piece = jnp.concatenate([sent, pick(target, (zl + k) % nz)], axis=0)
        pieces.append(shifted(piece, "zl", k))
    sent_rows = sent.shape[0]
    gathered = jnp.concatenate([piece[:sent_rows, :channels] for piece in pieces], axis=0)
    gathered_active = jnp.concatenate([piece[:sent_rows, channels:] for piece in pieces], axis=0)
    targets = wide(jnp.concatenate([piece[sent_rows:] for piece in pieces], axis=0))
    rc_grad, rc_narrow = reflect(
        partner,
        norm_gain,
        block_out,
        rc_perm,
        convolution_taps_weight,
        out_weight,
    )

    logits = dot(gathered, head, (1, 1))
    tracks = logits.shape[1]
    grouped = (nz * own_genes, exon_bins.shape[2], tracks)
    predicted = narrow(jax.nn.softplus(logits)).reshape(grouped)
    counted = lax.broadcasted_iota(jnp.int32, grouped[:2], 1) < targets[:, -1:].astype(jnp.int32)
    coverage = jnp.sum(jnp.where(counted[:, :, None], wide(predicted), 0.0), axis=1)
    wanted = targets[:, :tracks] + targets[:, tracks : 2 * tracks]
    spread_back = narrow(1.0 - wanted / (1.0 + coverage))
    logit_grad = narrow(
        wide(spread_back)[:, None, :] * jax.nn.sigmoid(logits).reshape(grouped)
    ).reshape(logits.shape)
    entry_grad = narrow(dot(logit_grad, head))
    back = entry_grad.reshape(nz, -1, channels)
    pieces = [shifted(back[k], "zl", -k) for k in range(1, nz)]
    back = narrow(wide(back[0]) + sum(wide(piece) for piece in pieces))
    back = jnp.concatenate([back, shifted(back, "zh", 1)], axis=0)
    back = jnp.concatenate([back] + [shifted(back, "y", -k) for k in range(1, ny)], axis=0)
    back_other = shifted(back, "core", 1)
    head_back = dot(pick_rows[:, : entries // 2], back) + dot(
        pick_rows[:, entries // 2 :], back_other
    )
    block_grad = narrow(head_back + rc_grad)

    half = channels // 2

    def turn(value):
        return jnp.where(core == 0, value, jnp.roll(value, half, axis=1))

    turned, turned_entries = turn(rc_narrow), turn(entry_grad)

    def share_of(cut):
        return dot(active, turned[:, cut], (0, 0)) + dot(
            gathered_active, turned_entries[:, cut], (0, 0)
        )

    piece = shifted(narrow(share_of(slice(half, None))), "core", 1)
    share = narrow(share_of(slice(0, half)) + wide(piece)).reshape(nx, -1, half)
    pieces = [shifted(pick(share, (x + k) % nx), "x", k) for k in range(1, nx)]
    share = wide(pick(share, x)) + sum(wide(piece) for piece in pieces)
    share = narrow(share).reshape(nz, -1, half)
    pieces = [shifted(pick(share, (zl + k) % nz), "zl", k) for k in range(1, nz)]
    share = narrow(wide(pick(share, zl)) + sum(wide(piece) for piece in pieces))
    share = narrow(
        (wide(share) + wide(shifted(share, "y", 2)))
        + (wide(shifted(share, "y", 1)) + wide(shifted(share, "y", 3)))
    )
    share = wide(share) + wide(shifted(share, "zh", 1))
    other = shifted(share, "core", 1)
    out_weight_grad = jnp.concatenate(
        [jnp.where(core == 0, share, other), jnp.where(core == 0, other, share)], axis=1
    )

    activation_gradient = narrow(dot(block_grad, out_weight, (1, 1)) * gelu_slope(convolved_sum))
    low, high = edge_rows(activation_gradient, DILATION_STEP)
    padded_gradient = jnp.concatenate([low, activation_gradient, high], axis=0)
    hidden_grad = jnp.zeros((count_of_rows, channels), jnp.float32)
    for tap in range(3):
        start = (2 - tap) * DILATION_STEP
        hidden_grad = hidden_grad + dot(
            padded_gradient[start : start + count_of_rows], convolution_taps_weight[tap], (1, 1)
        )
    widened = wide(after(rows, block_out))
    inverse = lax.rsqrt(jnp.mean(widened * widened, axis=-1, keepdims=True) + 1e-06)
    normed = widened * inverse * norm_gain
    normed_grad = hidden_grad * gelu_slope(normed) * norm_gain
    norm_back = inverse * normed_grad - widened * inverse**3 * jnp.mean(
        normed_grad * widened, axis=-1, keepdims=True
    )
    input_grad = narrow(wide(block_grad) + norm_back)
    return (input_grad[None], out_weight_grad)


def solution(mesh):
    cut = Mesh(mesh.devices.reshape(4, 2, 2, 4, 4), BINS + ("x", "zl"))
    batch = ("x", "zl")
    in_specs = (
        P(batch, BINS, None),
        P(),
        P(),
        P(),
        P(None, batch),
        P(),
        P(batch, None, None),
        P(batch, None),
        P(batch, None),
        P(batch, BINS, None),
    )
    out_specs = (P(batch, BINS, None), P(batch, None))
    return jax.shard_map(
        whole_step, mesh=cut, in_specs=in_specs, out_specs=out_specs, check_vma=False
    )
```

```python
import jax
import jax.numpy as jnp
from jax import lax
from jax.experimental import pallas as pl
from jax.experimental.pallas import tpu as pltpu
from jax.sharding import Mesh
from jax.sharding import PartitionSpec as P

DILATION_STEP = 16
BINS = ("y", "zh", "core")


def shifted(block, axis, shift):
    count = lax.axis_size(axis)
    return lax.ppermute(block, axis, [(i, (i + shift) % count) for i in range(count)])


def edge_rows(block, width):
    count = lax.axis_size(BINS)
    low = lax.ppermute(block[-width:], BINS, [(i, i + 1) for i in range(count - 1)])
    high = lax.ppermute(block[:width], BINS, [(i + 1, i) for i in range(count - 1)])
    return low, high


def pick(stack, index):
    return lax.dynamic_index_in_dim(stack, index, 0, keepdims=False)


def wide(value):
    return value.astype(jnp.float32)


def narrow(value):
    return value.astype(jnp.bfloat16)


def gelu_slope(argument):
    return (
        0.5 * (1.0 + jax.scipy.special.erf(argument * 0.7071067811865476))
        + argument * jnp.exp(-0.5 * argument * argument) * 0.3989422804014327
    )


def dot(left, right, over=(1, 0)):
    return lax.dot_general(
        left, right, (((over[0],), (over[1],)), ((), ())), preferred_element_type=jnp.float32
    )


INTERPRET = False
NORM_ROWS = 16


def gelu(argument):
    return 0.5 * argument * (1.0 + lax.erf(argument * 0.7071067811865476))


def block_columns(
    edge_ref, rows_ref, gain_ref, taps_hbm, out_hbm, taps_ref, out_ref, hidden_ref, active_ref,
    sems, put, emit, before_emit=None,
):
    taps_copy = pltpu.make_async_copy(taps_hbm, taps_ref, sems.at[0])
    out_copy = pltpu.make_async_copy(out_hbm, out_ref, sems.at[1])
    taps_copy.start()
    out_copy.start()
    count, channels = rows_ref.shape
    width = out_ref.shape[0]

    def normalize_some(value):
        value = wide(value)
        inverse = lax.rsqrt(jnp.mean(value * value, axis=-1, keepdims=True) + 1e-06)
        return narrow(gelu(value * inverse * gain_ref[...]))

    def normalize_rows(i, carry):
        start = pl.multiple_of(i * NORM_ROWS, NORM_ROWS)
        hidden_ref[pl.ds(start + DILATION_STEP, NORM_ROWS), :] = normalize_some(
            rows_ref[pl.ds(start, NORM_ROWS), :]
        )
        return carry

    hidden_ref[:DILATION_STEP, :] = normalize_some(edge_ref[:DILATION_STEP, :])
    hidden_ref[DILATION_STEP + count :, :] = normalize_some(edge_ref[DILATION_STEP:, :])
    lax.fori_loop(0, count // NORM_ROWS, normalize_rows, 0, unroll=2)
    taps_copy.wait()
    block = min(256, width)

    def columns(j):
        return pl.ds(pl.multiple_of(j * block, block), block)

    def convolve(j, carry):
        cut = columns(j)
        total = jnp.zeros((count, block), jnp.float32)
        for tap in range(3):
            total += dot(
                hidden_ref[tap * DILATION_STEP : tap * DILATION_STEP + count, :],
                taps_ref[tap, :, cut],
            )
        put(cut, total)
        return carry

    lax.fori_loop(0, width // block, convolve, 0)
    out_copy.wait()

    def project(j, carry):
        cut = columns(j)
        emit(cut, narrow(wide(rows_ref[:, cut]) + dot(active_ref[...], out_ref[:, cut])))
        return carry

    if before_emit:
        before_emit()
    lax.fori_loop(0, channels // block, project, 0)


def forward_kernel(
    base_ref, edge_ref, rows_ref, gain_ref, entry_ref, taps_hbm, out_hbm,
    kept_ref, sent_ref, active_ref, block_hbm, sum_hbm,
    taps_ref, out_ref, hidden_ref, pick_ref, block_ref, sum_ref, sems,
):
    count, channels = block_ref.shape
    sum_copy = pltpu.make_async_copy(sum_ref, sum_hbm, sems.at[2])
    block_copy = pltpu.make_async_copy(block_ref, block_hbm, sems.at[3])
    entries = entry_ref.shape[1]
    half = entries // 2
    row = base_ref[0] + lax.broadcasted_iota(jnp.int32, (count, entries), 0)
    pick_ref[...] = narrow(jnp.where(entry_ref[...] == row, 1.0, 0.0))
    core = base_ref[1]
    own = pick_ref.at[:, pl.ds(pl.multiple_of(core * half, half), half)]
    other = pick_ref.at[:, pl.ds(pl.multiple_of((1 - core) * half, half), half)]

    def put(cut, total):
        sum_ref[:, cut] = total
        active_ref[:, cut] = narrow(gelu(total))

    def emit(cut, part):
        block_ref[:, cut] = part
        sent_ref[:, cut] = narrow(dot(other[...], part, (0, 0)))
        kept_ref[:, cut] = narrow(dot(own[...], part, (0, 0)))

    block_columns(
        edge_ref, rows_ref, gain_ref, taps_hbm, out_hbm, taps_ref, out_ref, hidden_ref, active_ref,
        sems, put, emit, sum_copy.start,
    )
    block_copy.start()
    sent_ref[:, channels:] = narrow(dot(other[...], active_ref[...], (0, 0)))
    kept_ref[:, channels:] = narrow(dot(own[...], active_ref[...], (0, 0)))
    sum_copy.wait()
    block_copy.wait()


def reflect_kernel(
    edge_ref, rows_ref, gain_ref, own_ref, perm_ref, taps_hbm, out_hbm, wide_ref, narrow_ref,
    taps_ref, out_ref, hidden_ref, active_ref, partner_ref, mirror_ref, sems,
):
    count, channels = own_ref.shape

    def put(cut, total):
        active_ref[:, cut] = narrow(gelu(total))

    def emit(cut, part):
        partner_ref[:, cut] = part

    block_columns(
        edge_ref, rows_ref, gain_ref, taps_hbm, out_hbm, taps_ref, out_ref, hidden_ref, active_ref,
        sems, put, emit,
    )
    place = lax.broadcasted_iota(jnp.int32, (count, count), 0)
    other = lax.broadcasted_iota(jnp.int32, (count, count), 1)
    reversal = narrow(jnp.where(place + other == count - 1, 1.0, 0.0))
    mirror_ref[...] = narrow(dot(reversal, partner_ref[...]))
    wide_ref[...] = wide(own_ref[...])
    some = min(256, channels)

    def mix(j, carry):
        cut = pl.ds(pl.multiple_of(j * some, some), some)
        channel = j * some + lax.broadcasted_iota(jnp.int32, (some, channels), 0)
        chosen = narrow(jnp.where(perm_ref[...] == channel, 1.0, 0.0))
        wide_ref[...] -= 0.5 * dot(mirror_ref[:, cut], chosen)
        wide_ref[:, cut] -= 0.5 * dot(mirror_ref[...], chosen, (1, 1))
        return carry

    lax.fori_loop(0, channels // some, mix, 0)
    narrow_ref[...] = narrow(wide_ref[...])


def reflect(edges, rows, norm_gain, block_out, rc_perm, taps, out_weight):
    count, channels = block_out.shape
    vmem = pl.BlockSpec(memory_space=pltpu.VMEM)
    bf = jnp.bfloat16
    return pl.pallas_call(
        reflect_kernel,
        out_shape=[
            jax.ShapeDtypeStruct((count, channels), jnp.float32),
            jax.ShapeDtypeStruct((count, channels), bf),
        ],
        in_specs=[vmem] * 5 + [pl.BlockSpec(memory_space=pltpu.HBM)] * 2,
        out_specs=[vmem] * 2,
        scratch_shapes=[
            pltpu.VMEM(taps.shape, bf),
            pltpu.VMEM(out_weight.shape, bf),
            pltpu.VMEM((count + 2 * DILATION_STEP, channels), bf),
            pltpu.VMEM((count, out_weight.shape[0]), bf),
            pltpu.VMEM((count, channels), bf),
            pltpu.VMEM((count, channels), bf),
            pltpu.SemaphoreType.DMA((2,)),
        ],
        compiler_params=pltpu.CompilerParams(vmem_limit_bytes=20 << 20),
        cost_estimate=pl.CostEstimate(
            flops=count * channels * (8 * out_weight.shape[0] + 4 * channels),
            transcendentals=count * channels,
            bytes_accessed=2 * (taps.size + out_weight.size) + 10 * count * channels,
        ),
        name="reflect",
        interpret=INTERPRET,
    )(
        edges,
        rows,
        norm_gain[None, :],
        block_out,
        rc_perm[None, :],
        in_hbm(taps),
        in_hbm(out_weight),
    )


def hbm(shape, kind):
    return jax.ShapeDtypeStruct(shape, kind) if INTERPRET else pltpu.HBM(shape, kind)


def in_hbm(value):
    return value if INTERPRET else pltpu.with_memory_space_constraint(value, pltpu.HBM)


def forward(edges, rows, norm_gain, entry_bins, base, taps, out_weight):
    count, channels = rows.shape
    width = out_weight.shape[0]
    entries = entry_bins.shape[0]
    vmem = pl.BlockSpec(memory_space=pltpu.VMEM)
    bf = jnp.bfloat16
    payload = jax.ShapeDtypeStruct((entries // 2, channels + width), bf)
    return pl.pallas_call(
        forward_kernel,
        out_shape=[
            payload,
            payload,
            jax.ShapeDtypeStruct((count, width), bf),
            hbm((count, channels), bf),
            hbm((count, width), jnp.float32),
        ],
        in_specs=[pl.BlockSpec(memory_space=pltpu.SMEM), vmem, vmem, vmem, vmem]
        + [pl.BlockSpec(memory_space=pltpu.HBM)] * 2,
        out_specs=[vmem] * 3 + [pl.BlockSpec(memory_space=pltpu.HBM)] * 2,
        scratch_shapes=[
            pltpu.VMEM(taps.shape, bf),
            pltpu.VMEM(out_weight.shape, bf),
            pltpu.VMEM((count + 2 * DILATION_STEP, channels), bf),
            pltpu.VMEM((count, entries), bf),
            pltpu.VMEM((count, channels), bf),
            pltpu.VMEM((count, width), jnp.float32),
            pltpu.SemaphoreType.DMA((4,)),
        ],
        compiler_params=pltpu.CompilerParams(vmem_limit_bytes=20 << 20),
        cost_estimate=pl.CostEstimate(
            flops=2 * count * (4 * channels * width + entries * (channels + width)),
            transcendentals=count * (channels + width),
            bytes_accessed=2 * (taps.size + out_weight.size) + 8 * count * channels,
        ),
        name="forward",
        interpret=INTERPRET,
    )(
        base,
        edges,
        rows,
        norm_gain[None, :],
        entry_bins[None, :],
        in_hbm(taps),
        in_hbm(out_weight),
    )


def after(value, token):
    return lax.optimization_barrier((value, token))[0]


def gather_head(head_weight):
    mine = head_weight.T
    pieces = [shifted(mine, "x", k) for k in range(1, lax.axis_size("x"))]
    return jnp.concatenate([mine] + pieces, axis=0)


def target_rows(gene_target, own_strand, own_count, columns):
    nx, nz = lax.axis_size("x"), lax.axis_size("zl")
    x = lax.axis_index("x")
    genes, tracks = gene_target.shape
    odd = (lax.broadcasted_iota(jnp.int32, gene_target.shape, 1) & 1) == 1
    swapped = jnp.where(odd, jnp.roll(gene_target, 1, axis=1), jnp.roll(gene_target, -1, axis=1))
    flipped = jnp.where(own_strand[:, None] == 1, swapped, gene_target)
    parts = flipped.reshape(genes, nx, nz, tracks // (nx * nz))
    parts = jnp.transpose(parts, (1, 2, 0, 3))
    parts = jnp.concatenate([pick(parts, (x - k) % nx) for k in range(nx)], axis=2)
    rounded = lax.reduce_precision(parts, 8, 7)
    rest = columns - 2 * parts.shape[2]
    counts = jnp.broadcast_to(wide(own_count)[None, :, None], (nz, genes, rest))
    return narrow(jnp.concatenate([rounded, parts - rounded, counts], axis=2))


def listed_bins(exon_bins, exon_count):
    place = lax.broadcasted_iota(jnp.int32, exon_bins.shape, 1)
    return jnp.where(place < exon_count[:, None], exon_bins, -1)


def by_owner(entry_bins):
    ny, nh, nc = (lax.axis_size(a) for a in BINS)
    return entry_bins.reshape(ny, nh, nc, -1).transpose(2, 0, 1, 3).reshape(-1)


def by_distance(entry_bins):
    ny, nh, nc = (lax.axis_size(a) for a in BINS)
    y, zh, core = (lax.axis_index(a) for a in BINS)
    devices = ny * nh * nc
    owner = lax.iota(jnp.int32, devices)
    owner_core = (core + owner // (ny * nh)) % nc
    owner_y = (y + (owner // nh) % ny) % ny
    owner_zh = (zh + owner % nh) % nh
    owner = (owner_y * nh + owner_zh) * nc + owner_core
    entry_bins = entry_bins.reshape(devices, -1)
    chosen = owner[:, None] == lax.iota(jnp.int32, devices)[None, :]
    return jnp.sum(jnp.where(chosen[:, :, None], entry_bins[None], 0), axis=1).reshape(-1)


def whole_step(
    features,
    norm_gain,
    convolution_taps_weight,
    out_weight,
    head_weight,
    rc_perm,
    exon_bins,
    exon_count,
    gene_strand,
    gene_target,
):
    ny, nh, nc, nx, nz = (lax.axis_size(a) for a in ("y", "zh", "core", "x", "zl"))
    y, zh, core, x, zl = (lax.axis_index(a) for a in ("y", "zh", "core", "x", "zl"))
    bin_devices = ny * nh * nc
    bin_index = (y * nh + zh) * nc + core
    rows = features[0]
    count_of_rows, channels = rows.shape
    low, high = edge_rows(rows, DILATION_STEP)
    mirroring = [(i, bin_devices - 1 - i) for i in range(bin_devices)]
    partner = lax.ppermute(rows, BINS, mirroring)
    head = gather_head(head_weight)
    entry_bins = listed_bins(exon_bins[0], exon_count[0])
    entries = entry_bins.size
    edges = jnp.concatenate([low, high], axis=0)
    kept, sent, active, block_out, convolved_sum = forward(
        edges,
        rows,
        norm_gain,
        by_owner(entry_bins),
        jnp.stack([bin_index * count_of_rows, core]),
        convolution_taps_weight,
        out_weight,
    )

    sent = shifted(sent, "core", 1)
    sent = narrow(wide(kept) + wide(sent)).reshape(ny, -1, kept.shape[1])
    pieces = [shifted(pick(sent, (y + k) % ny), "y", k) for k in range(1, ny)]
    sent = narrow(wide(pick(sent, y)) + sum(wide(piece) for piece in pieces))
    sent = sent.reshape(nh, -1, kept.shape[1])
    partner_edges = lax.ppermute(after(edges, kept), BINS, mirroring)
    piece = shifted(pick(sent, 1 - zh), "zh", 1)
    sent = narrow(wide(pick(sent, zh)) + wide(piece))
    distant_bins = by_distance(after(entry_bins, block_out))
    positions = bin_index * count_of_rows + lax.iota(jnp.int32, count_of_rows)
    pick_rows = narrow(distant_bins[None, :] == positions[:, None])
    own_genes = exon_bins.shape[1] // bin_devices
    gene_strand, exon_count = after((gene_strand, exon_count), block_out)
    own_strand = lax.dynamic_slice_in_dim(gene_strand[0], bin_index * own_genes, own_genes, 0)
    own_count = lax.dynamic_slice_in_dim(exon_count[0], bin_index * own_genes, own_genes, 0)
    target = target_rows(
        after(gene_target[0], block_out), own_strand, own_count, kept.shape[1]
    )
    pieces = [jnp.concatenate([sent, pick(target, zl)], axis=0)]
    for k in range(1, nz):
        piece = jnp.concatenate([sent, pick(target, (zl + k) % nz)], axis=0)
        pieces.append(shifted(piece, "zl", k))
    sent_rows = sent.shape[0]
    gathered = jnp.concatenate([piece[:sent_rows, :channels] for piece in pieces], axis=0)
    gathered_active = jnp.concatenate([piece[:sent_rows, channels:] for piece in pieces], axis=0)
    targets = wide(jnp.concatenate([piece[sent_rows:] for piece in pieces], axis=0))
    rc_grad, rc_narrow = reflect(
        partner_edges,
        partner,
        norm_gain,
        block_out,
        rc_perm,
        convolution_taps_weight,
        out_weight,
    )

    logits = dot(gathered, head, (1, 1))
    tracks = logits.shape[1]
    grouped = (nz * own_genes, exon_bins.shape[2], tracks)
    predicted = narrow(jax.nn.softplus(logits)).reshape(grouped)
    counted = lax.broadcasted_iota(jnp.int32, grouped[:2], 1) < targets[:, -1:].astype(jnp.int32)
    coverage = jnp.sum(jnp.where(counted[:, :, None], wide(predicted), 0.0), axis=1)
    wanted = targets[:, :tracks] + targets[:, tracks : 2 * tracks]
    spread_back = narrow(1.0 - wanted / (1.0 + coverage))
    logit_grad = narrow(
        wide(spread_back)[:, None, :] * jax.nn.sigmoid(logits).reshape(grouped)
    ).reshape(logits.shape)
    entry_grad = narrow(dot(logit_grad, head))
    back = entry_grad.reshape(nz, -1, channels)
    pieces = [shifted(back[k], "zl", -k) for k in range(1, nz)]
    back = narrow(wide(back[0]) + sum(wide(piece) for piece in pieces))
    back = jnp.concatenate([back, shifted(back, "zh", 1)], axis=0)
    back = jnp.concatenate([back] + [shifted(back, "y", -k) for k in range(1, ny)], axis=0)
    back_other = shifted(back, "core", 1)
    head_back = dot(pick_rows[:, : entries // 2], back) + dot(
        pick_rows[:, entries // 2 :], back_other
    )
    block_grad = narrow(head_back + rc_grad)

    half = channels // 2

    def turn(value):
        return jnp.where(core == 0, value, jnp.roll(value, half, axis=1))

    turned, turned_entries = turn(rc_narrow), turn(entry_grad)

    def share_of(cut):
        return dot(active, turned[:, cut], (0, 0)) + dot(
            gathered_active, turned_entries[:, cut], (0, 0)
        )

    piece = shifted(narrow(share_of(slice(half, None))), "core", 1)
    share = narrow(share_of(slice(0, half)) + wide(piece)).reshape(nx, -1, half)
    pieces = [shifted(pick(share, (x + k) % nx), "x", k) for k in range(1, nx)]
    share = wide(pick(share, x)) + sum(wide(piece) for piece in pieces)
    share = narrow(share).reshape(nz, -1, half)
    pieces = [shifted(pick(share, (zl + k) % nz), "zl", k) for k in range(1, nz)]
    share = narrow(wide(pick(share, zl)) + sum(wide(piece) for piece in pieces))
    for flip in (1, 2):
        piece = lax.ppermute(share, "y", [(i, i ^ flip) for i in range(ny)])
        share = narrow(wide(share) + wide(piece))
    share = wide(share) + wide(shifted(share, "zh", 1))
    other = shifted(share, "core", 1)
    out_weight_grad = jnp.concatenate(
        [jnp.where(core == 0, share, other), jnp.where(core == 0, other, share)], axis=1
    )

    activation_gradient = narrow(dot(block_grad, out_weight, (1, 1)) * gelu_slope(convolved_sum))
    low, high = edge_rows(activation_gradient, DILATION_STEP)
    padded_gradient = jnp.concatenate([low, activation_gradient, high], axis=0)
    hidden_grad = jnp.zeros((count_of_rows, channels), jnp.float32)
    for tap in range(3):
        start = (2 - tap) * DILATION_STEP
        hidden_grad = hidden_grad + dot(
            padded_gradient[start : start + count_of_rows], convolution_taps_weight[tap], (1, 1)
        )
    widened = wide(after(rows, block_out))
    inverse = lax.rsqrt(jnp.mean(widened * widened, axis=-1, keepdims=True) + 1e-06)
    normed = widened * inverse * norm_gain
    normed_grad = hidden_grad * gelu_slope(normed) * norm_gain
    norm_back = inverse * normed_grad - widened * inverse**3 * jnp.mean(
        normed_grad * widened, axis=-1, keepdims=True
    )
    input_grad = narrow(wide(block_grad) + norm_back)
    return (input_grad[None], out_weight_grad)


def solution(mesh):
    cut = Mesh(mesh.devices.reshape(4, 2, 2, 4, 4), BINS + ("x", "zl"))
    batch = ("x", "zl")
    in_specs = (
        P(batch, BINS, None),
        P(),
        P(),
        P(),
        P(None, batch),
        P(),
        P(batch, None, None),
        P(batch, None),
        P(batch, None),
        P(batch, BINS, None),
    )
    out_specs = (P(batch, BINS, None), P(batch, None))
    return jax.shard_map(
        whole_step, mesh=cut, in_specs=in_specs, out_specs=out_specs, check_vma=False
    )
```
